32 devices in a mesh: dp: 4 (over y, x), tensor: 8 (over z, core).
Axes of the slice: x: 2, y: 2, z: 4, core: 2. Of those that a mesh axis runs over, the one named last changes fastest.
Arguments:
- tokens: bfloat16 [2048, 2048], P(('dp', 'tensor')), may hold values from -6 to 6
- cotangent: bfloat16 [2048, 2048], P(('dp', 'tensor')), may hold values from -6 to 6
- w_query: bfloat16 [2048, 2048], P(None, 'tensor'), may hold values from -0.125 to 0.125
- w_key: bfloat16 [2048, 2048], P(None, 'tensor'), may hold values from -0.125 to 0.125
- w_value: bfloat16 [2048, 2048], P(None, 'tensor'), may hold values from -0.125 to 0.125
- w_out: bfloat16 [2048, 2048], P('tensor'), may hold values from -0.125 to 0.125
- w_gate: bfloat16 [2048, 8192], P(None, 'tensor'), may hold values from -0.125 to 0.125
- w_up: bfloat16 [2048, 8192], P(None, 'tensor'), may hold values from -0.125 to 0.125
- w_down: bfloat16 [8192, 2048], P('tensor'), may hold values from -0.0625 to 0.0625
- q_gain: float32 [2048], P('tensor'), may hold values from 0.1 to 1.9
- k_gain: float32 [2048], P('tensor'), may hold values from 0.1 to 1.9
- attn_gain: float32 [2048], replicated, may hold values from 0.1 to 1.9
- ffn_gain: float32 [2048], replicated, may hold values from 0.1 to 1.9
Outputs:
- layer_out: float32 [2048, 2048], P(('dp', 'tensor'))
- grad_tokens: float32 [2048, 2048], P(('dp', 'tensor'))
- grad_w_query: float32 [2048, 2048], P(None, 'tensor')
- grad_w_key: float32 [2048, 2048], P(None, 'tensor')
- grad_w_value: float32 [2048, 2048], P(None, 'tensor')
- grad_w_out: float32 [2048, 2048], P('tensor')
- grad_w_gate: float32 [2048, 8192], P(None, 'tensor')
- grad_w_up: float32 [2048, 8192], P(None, 'tensor')
- grad_w_down: float32 [8192, 2048], P('tensor')
- grad_q_gain: float32 [2048], P('tensor')
- grad_k_gain: float32 [2048], P('tensor')
- grad_attn_gain: float32 [2048], replicated
- grad_ffn_gain: float32 [2048], replicated
The draws below stay inside these ranges and needn't reach their ends.
All inputs are finite; a program needn't handle non-finite values.
Results may differ from the reference program's by a relative error of at most 0.015.
Values may be sent and summed in bfloat16 or wider, within the bound.
No kernel may reach another device: no remote copies, remote signals or barrier semaphores. Data moves between devices by JAX's collectives and lax.ppermute only.
A program may use at most 192 MiB of HBM per device.

```python
import math
import jax
import jax.numpy as jnp
from jax import lax

D = 2048
H = 16
FF = 8192
HD = 128
SEQ = 256
TOKENS = 2048


def steps_of(stream_key, dims, split, least, largest):
    loudness = 1.0
    for position, blocks in split:
        heights = jax.random.uniform(jax.random.fold_in(jax.random.fold_in(stream_key, 6), position), (blocks,), jnp.float32, least / len(split), largest / len(split))
        loudness = loudness * jnp.repeat(jnp.exp(heights), dims[position] // blocks).reshape((-1,) + (1,) * (len(dims) - 1 - position))
    return loudness


def scatter_about(stream_key, extent, spread, reach, cuts=(), kind=jnp.bfloat16):
    values = spread * jax.random.normal(stream_key, extent, jnp.float32)
    if cuts:
        values = values * steps_of(stream_key, extent, cuts, -0.22, 0.18)
    return jnp.clip(values, -reach, reach).astype(kind)


def setup_inputs(seed: int = 0) -> dict:
    key_of = jax.random.split(jax.random.key(seed), 14)
    return {
        "tokens": scatter_about(key_of[0], (TOKENS, D), 1.0, 6.0, ((0, 32),)),
        "cotangent": scatter_about(key_of[1], (TOKENS, D), 1.0, 6.0, ((0, 32),)),
        "w_query": scatter_about(key_of[2], (D, D), D ** -0.5, 0.125, ((1, 8),)),
        "w_key": scatter_about(key_of[3], (D, D), D ** -0.5, 0.125, ((1, 8),)),
        "w_value": scatter_about(key_of[4], (D, D), D ** -0.5, 0.125, ((1, 8),)),
        "w_out": scatter_about(key_of[5], (D, D), D ** -0.5, 0.125, ((0, 8),)),
        "w_gate": scatter_about(key_of[6], (D, FF), D ** -0.5, 0.125, ((1, 8),)),
        "w_up": scatter_about(key_of[7], (D, FF), D ** -0.5, 0.125, ((1, 8),)),
        "w_down": scatter_about(key_of[8], (FF, D), FF ** -0.5, 0.0625, ((0, 8),)),
        "q_gain": jnp.clip(1.0 + 0.18 * jax.random.normal(key_of[9], (D,), jnp.float32), 0.1, 1.9),
        "k_gain": jnp.clip(1.0 + 0.18 * jax.random.normal(key_of[10], (D,), jnp.float32), 0.1, 1.9),
        "attn_gain": jnp.clip(1.0 + 0.18 * jax.random.normal(key_of[11], (D,), jnp.float32), 0.1, 1.9),
        "ffn_gain": jnp.clip(1.0 + 0.18 * jax.random.normal(key_of[12], (D,), jnp.float32), 0.1, 1.9),
    }


epsilon = 1e-06
rope_base = 500000.0

def rope_tables(length, head_width):
    half_width = head_width // 2
    exponent = jnp.arange(half_width, dtype=jnp.float32) * (2.0 / head_width)
    frequency = rope_base ** (-exponent)
    angles = jnp.arange(length, dtype=jnp.float32)[:, None] * frequency[None, :]
    cos_table = jnp.concatenate([jnp.cos(angles), jnp.cos(angles)], axis=1)
    sin_table = jnp.concatenate([jnp.sin(angles), jnp.sin(angles)], axis=1)
    return (cos_table[None, :, None, :], sin_table[None, :, None, :])

def rotate(field, cos_table, sin_table):
    half_width = field.shape[-1] // 2
    turned = jnp.concatenate([-field[..., half_width:], field[..., :half_width]], axis=-1)
    return field * cos_table + turned * sin_table

def unrotate(grad_field, cos_table, sin_table):
    half_width = grad_field.shape[-1] // 2
    moved = grad_field * sin_table
    back_part = jnp.concatenate([moved[..., half_width:], -moved[..., :half_width]], axis=-1)
    return grad_field * cos_table + back_part

def row_scale(matrix):
    return lax.rsqrt(lax.optimization_barrier(jnp.mean(matrix * matrix, axis=1, keepdims=True)) + epsilon)

def norm_back(grad_normed, normed, inverse):
    return inverse * (grad_normed - normed * lax.optimization_barrier(jnp.mean(grad_normed * normed, axis=1, keepdims=True)))

def product(left, right):
    return jnp.dot(left, right, preferred_element_type=jnp.float32)

def block_pass(x_block, dy_block, w_query, w_key, w_value, w_out, w_gate, w_up, w_down, q_gain, k_gain, attn_gain, ffn_gain):
    block_rows = x_block.shape[0]
    seq_count = block_rows // SEQ
    head_shape = (seq_count, SEQ, H, HD)
    cos_table, sin_table = rope_tables(SEQ, HD)
    score_scale = 1.0 / math.sqrt(HD)
    query = product(x_block, w_query)
    keys = product(x_block, w_key)
    values = product(x_block, w_value).astype(jnp.bfloat16)
    q_inverse = row_scale(query)
    k_inverse = row_scale(keys)
    q_normed = query * q_inverse
    k_normed = keys * k_inverse
    q_rot = rotate((q_normed * q_gain).reshape(head_shape), cos_table, sin_table).astype(jnp.bfloat16)
    k_rot = rotate((k_normed * k_gain).reshape(head_shape), cos_table, sin_table).astype(jnp.bfloat16)
    v_heads = values.reshape(head_shape)
    causal = jnp.arange(SEQ)[:, None] >= jnp.arange(SEQ)[None, :]
    scores = jnp.einsum('sqhd,skhd->shqk', q_rot.astype(jnp.float32), k_rot.astype(jnp.float32)) * score_scale
    scores = jnp.where(causal, scores, -1e+30)
    top_score = lax.optimization_barrier(jnp.max(scores, axis=3, keepdims=True))
    shifted = jnp.exp(scores - top_score)
    total = lax.optimization_barrier(jnp.sum(shifted, axis=3, keepdims=True))
    probs = (shifted / total).astype(jnp.bfloat16)
    log_total = top_score + jnp.log(total)
    attended = jnp.einsum('shqk,skhd->sqhd', probs.astype(jnp.float32), v_heads.astype(jnp.float32))
    attended = attended.astype(jnp.bfloat16).reshape(block_rows, D)
    attn_sum = product(attended, w_out)
    a_inverse = row_scale(attn_sum)
    a_normed = attn_sum * a_inverse
    mixed = x_block.astype(jnp.float32) + a_normed * attn_gain
    mixed_b = mixed.astype(jnp.bfloat16)
    gate = product(mixed_b, w_gate)
    up_proj = product(mixed_b, w_up)
    sigmoid_gate = jax.nn.sigmoid(gate)
    activated = gate * sigmoid_gate
    swiglu = (activated * up_proj).astype(jnp.bfloat16)
    ffn_sum = product(swiglu, w_down)
    m_inverse = row_scale(ffn_sum)
    m_normed = ffn_sum * m_inverse
    layer_out = mixed + m_normed * ffn_gain
    grad_out = dy_block.astype(jnp.float32)
    grad_ffn_gain = lax.optimization_barrier(jnp.sum(grad_out * m_normed, axis=0))
    grad_ffn = norm_back(grad_out * ffn_gain, m_normed, m_inverse).astype(jnp.bfloat16)
    grad_w_down = product(swiglu.T, grad_ffn)
    grad_swiglu = product(grad_ffn, w_down.T)
    grad_gate = (grad_swiglu * up_proj * sigmoid_gate * (1.0 + gate * (1.0 - sigmoid_gate))).astype(jnp.bfloat16)
    grad_up = (grad_swiglu * activated).astype(jnp.bfloat16)
    grad_w_gate = product(mixed_b.T, grad_gate)
    grad_w_up = product(mixed_b.T, grad_up)
    grad_mixed = grad_out + (product(grad_gate, w_gate.T) + product(grad_up, w_up.T))
    grad_attn_gain = lax.optimization_barrier(jnp.sum(grad_mixed * a_normed, axis=0))
    grad_attn = norm_back(grad_mixed * attn_gain, a_normed, a_inverse).astype(jnp.bfloat16)
    grad_w_out = product(attended.T, grad_attn)
    grad_attended = product(grad_attn, w_out.T).astype(jnp.bfloat16)
    grad_heads = grad_attended.reshape(head_shape).astype(jnp.float32)
    prob_back = jnp.where(causal, jnp.exp(scores - log_total), 0.0)
    grad_values = jnp.einsum('shqk,sqhd->skhd', probs.astype(jnp.float32), grad_heads).astype(jnp.bfloat16)
    grad_probs = jnp.einsum('sqhd,skhd->shqk', grad_heads, v_heads.astype(jnp.float32))
    inner = lax.optimization_barrier(jnp.sum(prob_back * grad_probs, axis=3, keepdims=True))
    grad_scores = (prob_back * (grad_probs - inner) * score_scale).astype(jnp.bfloat16)
    grad_qrot = jnp.einsum('shqk,skhd->sqhd', grad_scores.astype(jnp.float32), k_rot.astype(jnp.float32))
    grad_krot = jnp.einsum('shqk,sqhd->skhd', grad_scores.astype(jnp.float32), q_rot.astype(jnp.float32))
    grad_qn = unrotate(grad_qrot, cos_table, sin_table).reshape(block_rows, D)
    grad_kn = unrotate(grad_krot, cos_table, sin_table).reshape(block_rows, D)
    grad_q_gain = lax.optimization_barrier(jnp.sum(grad_qn * q_normed, axis=0))
    grad_k_gain = lax.optimization_barrier(jnp.sum(grad_kn * k_normed, axis=0))
    grad_query = norm_back(grad_qn * q_gain, q_normed, q_inverse).astype(jnp.bfloat16)
    grad_keys = norm_back(grad_kn * k_gain, k_normed, k_inverse).astype(jnp.bfloat16)
    grad_values = grad_values.reshape(block_rows, D)
    grad_w_query = product(x_block.T, grad_query)
    grad_w_key = product(x_block.T, grad_keys)
    grad_w_value = product(x_block.T, grad_values)
    grad_tokens = grad_mixed + (product(grad_query, w_query.T) + product(grad_keys, w_key.T) + product(grad_values, w_value.T))
    grads = (grad_w_query, grad_w_key, grad_w_value, grad_w_out, grad_w_gate, grad_w_up, grad_w_down, grad_q_gain, grad_k_gain, grad_attn_gain, grad_ffn_gain)
    return (layer_out, grad_tokens, grads)

def reference(tokens, cotangent, w_query, w_key, w_value, w_out, w_gate, w_up, w_down, q_gain, k_gain, attn_gain, ffn_gain):
    block_size = math.gcd(TOKENS, 16 * SEQ)
    block_count = TOKENS // block_size
    weights = (w_query, w_key, w_value, w_out, w_gate, w_up, w_down, q_gain, k_gain, attn_gain, ffn_gain)
    zeros = tuple((jnp.zeros(weight.shape, jnp.float32) for weight in weights))

    def advance(carry, pair):
        x_block, dy_block = pair
        layer_out, grad_tokens, grads = block_pass(x_block, dy_block, *weights)
        return (tuple((old + new for old, new in zip(carry, grads))), (layer_out, grad_tokens))
    totals, (outs, grads_in) = lax.scan(advance, zeros, (tokens.reshape(block_count, block_size, D), cotangent.reshape(block_count, block_size, D)))
    return (outs.reshape(TOKENS, D), grads_in.reshape(TOKENS, D), totals[0], totals[1], totals[2], totals[3], totals[4], totals[5], totals[6], totals[7], totals[8], totals[9], totals[10])
```

```python
import functools
import math

import jax
import jax.numpy as jnp
from jax import lax
from jax.experimental import pallas as pl
from jax.experimental.pallas import tpu as pltpu
from jax.sharding import PartitionSpec as P

HD = 128
SEQ = 256

epsilon = 1e-06
rope_base = 500000.0


def row_scale(matrix):
    return lax.rsqrt(jnp.mean(matrix * matrix, axis=1, keepdims=True) + epsilon)


def norm_back(grad_normed, normed, inverse):
    return inverse * (grad_normed - normed * jnp.mean(grad_normed * normed, axis=1, keepdims=True))


def product(left, right):
    return jnp.dot(left, right, preferred_element_type=jnp.float32)


def times_transposed(left, right):
    return lax.dot_general(
        left, right, (((1,), (1,)), ((), ())), preferred_element_type=jnp.float32
    )


def transposed_times(left, right):
    return lax.dot_general(
        left, right, (((0,), (0,)), ((), ())), preferred_element_type=jnp.float32
    )


def column(row, width):
    return jnp.broadcast_to(row, (width, row.shape[1])).T


def row_sums(matrix):
    return jnp.sum(matrix.T, axis=0, keepdims=True)


def sequence_rows(ref, s, chunk, half, lanes):
    top = ref[s * chunk : (s + 1) * chunk, lanes]
    bottom = ref[half + s * chunk : half + (s + 1) * chunk, lanes]
    return jnp.concatenate([top, bottom], axis=0)


def store_rows(ref, s, chunk, half, lanes, value):
    ref[s * chunk : (s + 1) * chunk, lanes] = value[:chunk]
    ref[half + s * chunk : half + (s + 1) * chunk, lanes] = value[chunk:]


def sequence_row(ref, i, s, chunk, half):
    return jnp.concatenate(
        [
            ref[i : i + 1, s * chunk : (s + 1) * chunk],
            ref[i : i + 1, half + s * chunk : half + (s + 1) * chunk],
        ],
        axis=1,
    )


def causal_mask(pos_ref, s, chunk, half):
    key_pos = sequence_row(pos_ref, 0, s, chunk, half)
    length = 2 * chunk
    key_all = jnp.broadcast_to(key_pos, (length, length))
    return key_all.T >= key_all


def attend_kernel(
    model_width,
    query_ref,
    keys_ref,
    values_ref,
    squares_ref,
    q_gain_ref,
    k_gain_ref,
    cos_ref,
    sin_ref,
    pos_ref,
    attended_ref,
    q_rot_ref,
    k_rot_ref,
):
    rows, width = query_ref.shape
    half = rows // 2
    chunk = SEQ // 2
    for s in range(rows // SEQ):
        every = slice(None)
        cos = sequence_rows(cos_ref, s, chunk, half, every)
        sin = sequence_rows(sin_ref, s, chunk, half, every)
        mask = causal_mask(pos_ref, s, chunk, half)
        q_inv = column(
            lax.rsqrt(sequence_row(squares_ref, 0, s, chunk, half) / model_width + epsilon), HD
        )
        k_inv = column(
            lax.rsqrt(sequence_row(squares_ref, 1, s, chunk, half) / model_width + epsilon), HD
        )
        for h in range(width // HD):
            lanes = slice(h * HD, (h + 1) * HD)
            q = sequence_rows(query_ref, s, chunk, half, lanes) * q_inv * q_gain_ref[:, lanes]
            k = sequence_rows(keys_ref, s, chunk, half, lanes) * k_inv * k_gain_ref[:, lanes]
            q = (q * cos + pltpu.roll(q, HD // 2, 1) * sin).astype(jnp.bfloat16)
            k = (k * cos + pltpu.roll(k, HD // 2, 1) * sin).astype(jnp.bfloat16)
            store_rows(q_rot_ref, s, chunk, half, lanes, q)
            store_rows(k_rot_ref, s, chunk, half, lanes, k)
            scores = times_transposed(q, k) * (1.0 / math.sqrt(HD))
            scores = jnp.where(mask, scores, -1e30)
            shifted = jnp.exp(scores - jnp.max(scores, axis=1, keepdims=True))
            probs = (shifted / jnp.sum(shifted, axis=1, keepdims=True)).astype(jnp.bfloat16)
            v = sequence_rows(values_ref, s, chunk, half, lanes)
            store_rows(
                attended_ref, s, chunk, half, lanes, product(probs, v).astype(jnp.bfloat16)
            )


def attend(query, keys, values, squares, q_gain, k_gain, tables, model_width):
    rows, width = query.shape
    out = jax.ShapeDtypeStruct((rows, width), jnp.bfloat16)
    return pl.pallas_call(
        functools.partial(attend_kernel, model_width),
        out_shape=(out, out, out),
        name="attend",
        cost_estimate=pl.CostEstimate(
            flops=4 * rows * SEQ * width,
            bytes_accessed=16 * rows * width,
            transcendentals=rows * SEQ * width // HD,
        ),
    )(query, keys, values, squares, q_gain[None, :], k_gain[None, :], *tables)


def attend_back_kernel(
    model_width,
    grad_ref,
    q_rot_ref,
    k_rot_ref,
    values_ref,
    query_ref,
    keys_ref,
    squares_ref,
    q_gain_ref,
    k_gain_ref,
    cos_ref,
    sin_ref,
    pos_ref,
    grad_values_ref,
    grad_q_ref,
    grad_k_ref,
    inner_ref,
    gain_ref,
):
    rows, width = query_ref.shape
    half = rows // 2
    chunk = SEQ // 2
    scale = 1.0 / math.sqrt(HD)
    gain_ref[...] = jnp.zeros_like(gain_ref)
    for s in range(rows // SEQ):
        every = slice(None)
        cos = sequence_rows(cos_ref, s, chunk, half, every)
        sin = sequence_rows(sin_ref, s, chunk, half, every)
        mask = causal_mask(pos_ref, s, chunk, half)
        q_inv = column(
            lax.rsqrt(sequence_row(squares_ref, 0, s, chunk, half) / model_width + epsilon), HD
        )
        k_inv = column(
            lax.rsqrt(sequence_row(squares_ref, 1, s, chunk, half) / model_width + epsilon), HD
        )
        q_inner = jnp.zeros((1, SEQ), jnp.float32)
        k_inner = jnp.zeros((1, SEQ), jnp.float32)
        for h in range(width // HD):
            lanes = slice(h * HD, (h + 1) * HD)
            q = sequence_rows(q_rot_ref, s, chunk, half, lanes)
            k = sequence_rows(k_rot_ref, s, chunk, half, lanes)
            v = sequence_rows(values_ref, s, chunk, half, lanes)
            g = sequence_rows(grad_ref, s, chunk, half, lanes)
            scores = times_transposed(q, k) * scale
            scores = jnp.where(mask, scores, -1e30)
            shifted = jnp.exp(scores - jnp.max(scores, axis=1, keepdims=True))
            probs = shifted / jnp.sum(shifted, axis=1, keepdims=True)
            grad_v = transposed_times(probs.astype(jnp.bfloat16), g).astype(jnp.bfloat16)
            store_rows(grad_values_ref, s, chunk, half, lanes, grad_v)
            grad_probs = times_transposed(g, v)
            inner = jnp.sum(probs * grad_probs, axis=1, keepdims=True)
            grad_scores = (probs * (grad_probs - inner) * scale).astype(jnp.bfloat16)
            grad_q = product(grad_scores, k)
            grad_k = transposed_times(grad_scores, q)
            grad_q = grad_q * cos - pltpu.roll(grad_q, HD // 2, 1) * sin
            grad_k = grad_k * cos - pltpu.roll(grad_k, HD // 2, 1) * sin
            q_part = grad_q * (sequence_rows(query_ref, s, chunk, half, lanes) * q_inv)
            k_part = grad_k * (sequence_rows(keys_ref, s, chunk, half, lanes) * k_inv)
            gain_ref[0:1, lanes] += jnp.sum(q_part, axis=0, keepdims=True)
            gain_ref[1:2, lanes] += jnp.sum(k_part, axis=0, keepdims=True)
            q_inner += row_sums(q_part * q_gain_ref[:, lanes])
            k_inner += row_sums(k_part * k_gain_ref[:, lanes])
            store_rows(grad_q_ref, s, chunk, half, lanes, grad_q * q_gain_ref[:, lanes])
            store_rows(grad_k_ref, s, chunk, half, lanes, grad_k * k_gain_ref[:, lanes])
        for i, value in ((0, q_inner), (1, k_inner)):
            inner_ref[i : i + 1, s * chunk : (s + 1) * chunk] = value[:, :chunk]
            inner_ref[i : i + 1, half + s * chunk : half + (s + 1) * chunk] = value[:, chunk:]


def attend_back(
    grad_attended, q_rot, k_rot, values, query, keys, squares, q_gain, k_gain, tables, model_width
):
    rows, width = query.shape
    wide = jax.ShapeDtypeStruct((rows, width), jnp.float32)
    return pl.pallas_call(
        functools.partial(attend_back_kernel, model_width),
        out_shape=(
            jax.ShapeDtypeStruct((rows, width), jnp.bfloat16),
            wide,
            wide,
            jax.ShapeDtypeStruct((2, rows), jnp.float32),
            jax.ShapeDtypeStruct((2, width), jnp.float32),
        ),
        name="attend_back",
        cost_estimate=pl.CostEstimate(
            flops=10 * rows * SEQ * width,
            bytes_accessed=26 * rows * width,
            transcendentals=rows * SEQ * width // HD,
        ),
    )(
        grad_attended,
        q_rot,
        k_rot,
        values,
        query,
        keys,
        squares,
        q_gain[None, :],
        k_gain[None, :],
        *tables,
    )


def finish_kernel(
    model_width, query_ref, keys_ref, grad_q_ref, grad_k_ref, squares_ref, inner_ref, out_ref
):
    rows, width = query_ref.shape
    for i, source, target in ((0, query_ref, grad_q_ref), (1, keys_ref, grad_k_ref)):
        inverse = column(lax.rsqrt(squares_ref[i : i + 1, :] / model_width + epsilon), HD)
        inner = column(inner_ref[i : i + 1, :] / model_width, HD)
        for h in range(width // HD):
            lanes = slice(h * HD, (h + 1) * HD)
            normed = source[:, lanes] * inverse
            value = inverse * (target[:, lanes] - normed * inner)
            start = i * width + h * HD
            out_ref[:, start : start + HD] = value.astype(jnp.bfloat16)


def finish(query, keys, grad_q, grad_k, squares, inner, model_width):
    rows, width = query.shape
    return pl.pallas_call(
        functools.partial(finish_kernel, model_width),
        out_shape=jax.ShapeDtypeStruct((rows, 2 * width), jnp.bfloat16),
        name="finish",
        cost_estimate=pl.CostEstimate(
            flops=10 * rows * width, bytes_accessed=20 * rows * width, transcendentals=0
        ),
    )(query, keys, grad_q, grad_k, squares, inner)


def empty(shape, dtype):
    return pl.pallas_call(
        lambda out_ref: None,
        out_shape=jax.ShapeDtypeStruct(shape, dtype),
        out_specs=pl.BlockSpec(memory_space=pl.ANY),
        name="empty",
    )()


def build(dp_size, tensor_size):
    pairs = tensor_size // 2

    def swap(value, axis, mask):
        size = dp_size if axis == "dp" else tensor_size
        return lax.ppermute(value, axis, [(i, i ^ mask) for i in range(size)])

    def tensor_gather(own):
        parts = [own] + [swap(own, "tensor", 2 * k) for k in range(1, pairs)]
        near = jnp.concatenate(parts, axis=0)
        return jnp.concatenate([near, swap(near, "tensor", 1)], axis=0)

    def tensor_scatter(partial_of, rows):
        half = rows // 2
        far = swap(partial_of(half, rows).astype(jnp.bfloat16), "tensor", 1)
        near = partial_of(0, half) + far.astype(jnp.float32)
        count = half // pairs
        total = near[:count]
        for k in range(1, pairs):
            block = near[k * count : (k + 1) * count].astype(jnp.bfloat16)
            total = total + swap(block, "tensor", 2 * k).astype(jnp.float32)
        return total

    def tensor_sum(value):
        value = value + swap(value, "tensor", 1)
        return tree_sum(value, "tensor", pairs, 2)

    def row_sum(value):
        rows = value.shape[1]
        blocks = value.reshape(2, tensor_size, rows // tensor_size)
        blocks = blocks.transpose(1, 0, 2).reshape(tensor_size, -1)

        def reordered(other, mask):
            order = []
            for i in range(tensor_size):
                wanted = (2 * (i % pairs) + i // pairs) ^ mask
                order.append((wanted % 2) * pairs + wanted // 2)
            return jnp.concatenate([other[j : j + 1] for j in order], axis=0)

        total = blocks + reordered(swap(blocks, "tensor", 1), 1)
        others = [reordered(swap(total, "tensor", 2 * k), 2 * k) for k in range(1, pairs)]
        total = sum(others, total)
        total = total.reshape(tensor_size, 2, rows // tensor_size).transpose(1, 0, 2)
        return total.reshape(2, rows)

    def tree_sum(value, axis, count, step):
        values = [value] + [swap(value, axis, step * k) for k in range(1, count)]
        while len(values) > 1:
            values = [values[i] + values[i + 1] for i in range(0, len(values), 2)]
        return values[0]

    def dp_parts(own):
        rows = own.shape[0]
        if dp_size == 4:
            x_part = swap(own, "dp", 1)
            y_part = swap(own, "dp", 2)
            cut = rows // 2
            top = swap(x_part[:cut], "dp", 2)
            bottom = swap(y_part[cut:], "dp", 1)
            return [(1, 0, x_part), (2, 0, y_part), (3, 0, top), (3, cut, bottom)]
        return [(j, 0, swap(own, "dp", j)) for j in range(1, dp_size)]

    def place(buffer, value, mask, row, rows):
        start = (lax.axis_index("dp") ^ mask) * rows + row
        return lax.dynamic_update_slice(buffer, value, (start, jnp.zeros_like(start)))

    def dp_gather(own):
        rows, width = own.shape
        buffer = empty((dp_size * rows, width), own.dtype)
        buffer = place(buffer, own, 0, 0, rows)
        for mask, row, value in dp_parts(own):
            buffer = place(buffer, value, mask, row, rows)
        return buffer

    def dp_gather_shared(own):
        rows, width = own.shape
        half = rows // 2
        buffer = empty((dp_size * rows, width), own.dtype)
        buffer = place(buffer, own, 0, 0, rows)
        for mask, row, value in dp_parts(own[:half]):
            buffer = place(buffer, value, mask, row, rows)
            buffer = place(buffer, swap(value, "tensor", 1), mask, half + row, rows)
        return buffer

    def dp_sum(matrix):
        rows = matrix.shape[0] // dp_size
        rounded = matrix.astype(jnp.bfloat16)
        me = lax.axis_index("dp")
        zero = jnp.zeros_like(me)
        own = lax.dynamic_slice_in_dim(matrix, me * rows, rows, 0)
        total = own
        for j in range(1, dp_size):
            piece = lax.dynamic_slice_in_dim(rounded, (me ^ j) * rows, rows, 0)
            total = total + swap(piece, "dp", j).astype(jnp.float32)
        total = lax.optimization_barrier(total.astype(jnp.bfloat16))
        result = jnp.zeros(matrix.shape, jnp.float32)
        for j in range(dp_size):
            piece = total if j == 0 else swap(total, "dp", j)
            result = lax.dynamic_update_slice(
                result, piece.astype(jnp.float32), ((me ^ j) * rows, zero)
            )
        return result

    def positions(rows):
        count = rows // tensor_size
        index = jnp.arange(rows, dtype=jnp.int32)
        block = index // count
        mask = 2 * (block % pairs) + block // pairs
        owner = lax.axis_index("tensor").astype(jnp.int32) ^ mask
        return (owner * count + index % count) % SEQ

    def tables_of(rows):
        pos = positions(rows)
        half_width = HD // 2
        exponent = jnp.arange(half_width, dtype=jnp.float32) * (2.0 / HD)
        frequency = rope_base ** (-exponent)
        angles = pos.astype(jnp.float32)[:, None] * frequency[None, :]
        cos, sin = jnp.cos(angles), jnp.sin(angles)
        return (
            jnp.concatenate([cos, cos], axis=1),
            jnp.concatenate([-sin, sin], axis=1),
            pos[None, :],
        )

    def shards(
        tokens,
        cotangent,
        w_query,
        w_key,
        w_value,
        w_out,
        w_gate,
        w_up,
        w_down,
        q_gain,
        k_gain,
        attn_gain,
        ffn_gain,
    ):
        model_width = tokens.shape[1]
        rows = tokens.shape[0] * tensor_size
        width = w_query.shape[1]
        units = w_gate.shape[1]
        tables = tables_of(rows)

        gathered = tensor_gather(tokens)
        query = product(gathered, w_query)
        keys = product(gathered, w_key)
        squares = row_sum(
            jnp.stack([jnp.sum(query * query, axis=1), jnp.sum(keys * keys, axis=1)])
        )
        values = product(gathered, w_value).astype(jnp.bfloat16)
        attended, q_rot, k_rot = attend(
            query, keys, values, squares, q_gain, k_gain, tables, model_width
        )
        attn_rows = tensor_scatter(lambda a, b: product(attended[a:b], w_out), rows)
        a_inverse = row_scale(attn_rows)
        a_normed = attn_rows * a_inverse
        mixed = tokens.astype(jnp.float32) + a_normed * attn_gain
        mixed_b = tensor_gather(mixed.astype(jnp.bfloat16))
        gate = product(mixed_b, w_gate)
        up_proj = product(mixed_b, w_up)
        sigmoid_gate = jax.nn.sigmoid(gate)
        activated = gate * sigmoid_gate
        swiglu = (activated * up_proj).astype(jnp.bfloat16)
        ffn_rows = tensor_scatter(lambda a, b: product(swiglu[a:b], w_down), rows)
        m_inverse = row_scale(ffn_rows)
        m_normed = ffn_rows * m_inverse
        layer_out = mixed + m_normed * ffn_gain
        grad_out = cotangent.astype(jnp.float32)
        ffn_gain_part = jnp.sum(grad_out * m_normed, axis=0)
        grad_ffn = tensor_gather(
            norm_back(grad_out * ffn_gain, m_normed, m_inverse).astype(jnp.bfloat16)
        )
        grad_swiglu = times_transposed(grad_ffn, w_down)
        grad_gate = (
            grad_swiglu * up_proj * sigmoid_gate * (1.0 + gate * (1.0 - sigmoid_gate))
        ).astype(jnp.bfloat16)
        grad_up = (grad_swiglu * activated).astype(jnp.bfloat16)
        grad_mixed = grad_out + tensor_scatter(
            lambda a, b: times_transposed(grad_gate[a:b], w_gate)
            + times_transposed(grad_up[a:b], w_up),
            rows,
        )
        attn_gain_part = jnp.sum(grad_mixed * a_normed, axis=0)
        grad_attn = tensor_gather(
            norm_back(grad_mixed * attn_gain, a_normed, a_inverse).astype(jnp.bfloat16)
        )
        grad_attended = times_transposed(grad_attn, w_out).astype(jnp.bfloat16)
        grad_values, grad_q, grad_k, inner, gain_parts = attend_back(
            grad_attended,
            q_rot,
            k_rot,
            values,
            query,
            keys,
            squares,
            q_gain,
            k_gain,
            tables,
            model_width,
        )
        inner = row_sum(inner)
        grad_qk = finish(query, keys, grad_q, grad_k, squares, inner, model_width)
        grad_tokens = grad_mixed + tensor_scatter(
            lambda a, b: times_transposed(grad_qk[a:b, :width], w_query)
            + times_transposed(grad_qk[a:b, width:], w_key)
            + times_transposed(grad_values[a:b], w_value),
            rows,
        )

        tokens_all = dp_gather_shared(gathered)
        mixed_all = dp_gather_shared(mixed_b)
        swiglu_all = dp_gather(swiglu)
        grad_ffn_all = dp_gather_shared(grad_ffn)
        grad_w_down = transposed_times(swiglu_all, grad_ffn_all)
        gate_up_all = dp_gather(jnp.concatenate([grad_gate, grad_up], axis=1))
        grad_w_gate = transposed_times(mixed_all, gate_up_all[:, :units])
        grad_w_up = transposed_times(mixed_all, gate_up_all[:, units:])
        grad_w_out = dp_sum(transposed_times(attended, grad_attn))
        grad_values_all = dp_gather(grad_values)
        grad_w_value = transposed_times(tokens_all, grad_values_all)
        grad_qk_all = dp_gather(grad_qk)
        grad_w_query = transposed_times(tokens_all, grad_qk_all[:, :width])
        grad_w_key = transposed_times(tokens_all, grad_qk_all[:, width:])
        post_gains = tensor_sum(jnp.stack([attn_gain_part, ffn_gain_part]))
        gains = tree_sum(
            jnp.concatenate([post_gains.reshape(-1), gain_parts.reshape(-1)]), "dp", dp_size, 1
        )
        return (
            layer_out,
            grad_tokens,
            grad_w_query,
            grad_w_key,
            grad_w_value,
            grad_w_out,
            grad_w_gate,
            grad_w_up,
            grad_w_down,
            gains[2 * model_width : 2 * model_width + width],
            gains[2 * model_width + width :],
            gains[:model_width],
            gains[model_width : 2 * model_width],
        )

    return shards


def solution(mesh):
    placed = (
        P(("dp", "tensor"), None),
        P(("dp", "tensor"), None),
        P(None, "tensor"),
        P(None, "tensor"),
        P(None, "tensor"),
        P("tensor", None),
        P(None, "tensor"),
        P(None, "tensor"),
        P("tensor", None),
        P("tensor"),
        P("tensor"),
        P(),
        P(),
    )
    return jax.shard_map(
        build(mesh.shape["dp"], mesh.shape["tensor"]),
        mesh=mesh,
        in_specs=placed,
        out_specs=(
            P(("dp", "tensor"), None),
            P(("dp", "tensor"), None),
            P(None, "tensor"),
            P(None, "tensor"),
            P(None, "tensor"),
            P("tensor", None),
            P(None, "tensor"),
            P(None, "tensor"),
            P("tensor", None),
            P("tensor"),
            P("tensor"),
            P(),
            P(),
        ),
        check_vma=False,
    )
```

```python
import functools
import math

import jax
import jax.numpy as jnp
from jax import lax
from jax.experimental import pallas as pl
from jax.experimental.pallas import tpu as pltpu
from jax.sharding import PartitionSpec as P

HD = 128
SEQ = 256

epsilon = 1e-06
rope_base = 500000.0

MIB = 1 << 20


def row_scale(matrix):
    return lax.rsqrt(jnp.mean(matrix * matrix, axis=1, keepdims=True) + epsilon)


def norm_back(grad_normed, normed, inverse):
    return inverse * (grad_normed - normed * jnp.mean(grad_normed * normed, axis=1, keepdims=True))


def product(left, right):
    return jnp.dot(left, right, preferred_element_type=jnp.float32)


def times_transposed(left, right):
    return lax.dot_general(
        left, right, (((1,), (1,)), ((), ())), preferred_element_type=jnp.float32
    )


def transposed_times(left, right):
    return lax.dot_general(
        left, right, (((0,), (0,)), ((), ())), preferred_element_type=jnp.float32
    )


def column(row, width):
    return jnp.broadcast_to(row, (width, row.shape[1])).T


def row_sums(matrix):
    return jnp.sum(matrix.T, axis=0, keepdims=True)


def sequence_rows(ref, s, chunk, half, lanes):
    top = ref[s * chunk : (s + 1) * chunk, lanes]
    bottom = ref[half + s * chunk : half + (s + 1) * chunk, lanes]
    return jnp.concatenate([top, bottom], axis=0)


def store_rows(ref, s, chunk, half, lanes, value):
    ref[s * chunk : (s + 1) * chunk, lanes] = value[:chunk]
    ref[half + s * chunk : half + (s + 1) * chunk, lanes] = value[chunk:]


def block_row(ref, i, blocks):
    count = ref.shape[1] // 2
    return jnp.concatenate(
        [ref[b : b + 1, i * count : (i + 1) * count] for b in blocks], axis=1
    )


def sequence_blocks(ref, s, chunk):
    count = ref.shape[1] // 2
    steps = chunk // count
    pairs = ref.shape[0] // 2
    return [h * pairs + s * steps + k for h in range(2) for k in range(steps)]


def store_blocks(ref, i, blocks, row):
    count = ref.shape[1] // 2
    for j, b in enumerate(blocks):
        ref[b : b + 1, i * count : (i + 1) * count] = row[:, j * count : (j + 1) * count]


def causal_mask(pos_ref, s, chunk, half):
    key_pos = jnp.concatenate(
        [
            pos_ref[:, s * chunk : (s + 1) * chunk],
            pos_ref[:, half + s * chunk : half + (s + 1) * chunk],
        ],
        axis=1,
    )
    length = 2 * chunk
    key_all = jnp.broadcast_to(key_pos, (length, length))
    return key_all.T >= key_all


def attend_kernel(model_width, orders, *refs):
    parts = refs[: len(orders) + 1]
    (
        query_ref,
        keys_ref,
        values_ref,
        q_gain_ref,
        k_gain_ref,
        cos_ref,
        sin_ref,
        pos_ref,
        attended_ref,
        q_rot_ref,
        k_rot_ref,
        squares_ref,
    ) = refs[len(parts) :]
    for i, row in enumerate(summed_blocks(parts, orders)):
        squares_ref[i : i + 1, :] = row
    rows, width = query_ref.shape
    half = rows // 2
    chunk = SEQ // 2
    for s in range(rows // SEQ):
        every = slice(None)
        cos = sequence_rows(cos_ref, s, chunk, half, every)
        sin = sequence_rows(sin_ref, s, chunk, half, every)
        mask = causal_mask(pos_ref, s, chunk, half)
        blocks = sequence_blocks(squares_ref, s, chunk)
        q_inv = column(lax.rsqrt(block_row(squares_ref, 0, blocks) / model_width + epsilon), HD)
        k_inv = column(lax.rsqrt(block_row(squares_ref, 1, blocks) / model_width + epsilon), HD)
        for h in range(width // HD):
            lanes = slice(h * HD, (h + 1) * HD)
            q = sequence_rows(query_ref, s, chunk, half, lanes) * q_inv * q_gain_ref[:, lanes]
            k = sequence_rows(keys_ref, s, chunk, half, lanes) * k_inv * k_gain_ref[:, lanes]
            q = (q * cos + pltpu.roll(q, HD // 2, 1) * sin).astype(jnp.bfloat16)
            k = (k * cos + pltpu.roll(k, HD // 2, 1) * sin).astype(jnp.bfloat16)
            store_rows(q_rot_ref, s, chunk, half, lanes, q)
            store_rows(k_rot_ref, s, chunk, half, lanes, k)
            scores = times_transposed(q, k) * (1.0 / math.sqrt(HD))
            scores = jnp.where(mask, scores, -1e30)
            shifted = jnp.exp(scores - jnp.max(scores, axis=1, keepdims=True))
            probs = (shifted / jnp.sum(shifted, axis=1, keepdims=True)).astype(jnp.bfloat16)
            v = sequence_rows(values_ref, s, chunk, half, lanes)
            store_rows(
                attended_ref, s, chunk, half, lanes, product(probs, v).astype(jnp.bfloat16)
            )


def attend(query, keys, values, squares, orders, q_gain, k_gain, tables, model_width):
    rows, width = query.shape
    out = jax.ShapeDtypeStruct((rows, width), jnp.bfloat16)
    return pl.pallas_call(
        functools.partial(attend_kernel, model_width, orders),
        out_shape=(
            out,
            out,
            out,
            jax.ShapeDtypeStruct(squares[0].shape, jnp.float32),
        ),
        name="attend",
        compiler_params=pltpu.CompilerParams(vmem_limit_bytes=16 * MIB),
        cost_estimate=pl.CostEstimate(
            flops=4 * rows * SEQ * width,
            bytes_accessed=16 * rows * width,
            transcendentals=rows * SEQ * width // HD,
        ),
    )(*squares, query, keys, values, q_gain[None, :], k_gain[None, :], *tables)


def attend_back_kernel(
    model_width,
    grad_ref,
    q_rot_ref,
    k_rot_ref,
    values_ref,
    query_ref,
    keys_ref,
    squares_ref,
    q_gain_ref,
    k_gain_ref,
    cos_ref,
    sin_ref,
    pos_ref,
    grad_values_ref,
    grad_q_ref,
    grad_k_ref,
    inner_ref,
    gain_ref,
):
    rows, width = query_ref.shape
    half = rows // 2
    chunk = SEQ // 2
    scale = 1.0 / math.sqrt(HD)
    gain_ref[...] = jnp.zeros_like(gain_ref)
    for s in range(rows // SEQ):
        every = slice(None)
        cos = sequence_rows(cos_ref, s, chunk, half, every)
        sin = sequence_rows(sin_ref, s, chunk, half, every)
        mask = causal_mask(pos_ref, s, chunk, half)
        blocks = sequence_blocks(squares_ref, s, chunk)
        q_inv = column(lax.rsqrt(block_row(squares_ref, 0, blocks) / model_width + epsilon), HD)
        k_inv = column(lax.rsqrt(block_row(squares_ref, 1, blocks) / model_width + epsilon), HD)
        q_inner = jnp.zeros((1, SEQ), jnp.float32)
        k_inner = jnp.zeros((1, SEQ), jnp.float32)
        for h in range(width // HD):
            lanes = slice(h * HD, (h + 1) * HD)
            q = sequence_rows(q_rot_ref, s, chunk, half, lanes)
            k = sequence_rows(k_rot_ref, s, chunk, half, lanes)
            v = sequence_rows(values_ref, s, chunk, half, lanes)
            g = sequence_rows(grad_ref, s, chunk, half, lanes)
            scores = times_transposed(q, k) * scale
            scores = jnp.where(mask, scores, -1e30)
            shifted = jnp.exp(scores - jnp.max(scores, axis=1, keepdims=True))
            probs = shifted / jnp.sum(shifted, axis=1, keepdims=True)
            grad_v = transposed_times(probs.astype(jnp.bfloat16), g).astype(jnp.bfloat16)
            store_rows(grad_values_ref, s, chunk, half, lanes, grad_v)
            grad_probs = times_transposed(g, v)
            inner = jnp.sum(probs * grad_probs, axis=1, keepdims=True)
            grad_scores = (probs * (grad_probs - inner) * scale).astype(jnp.bfloat16)
            grad_q = product(grad_scores, k)
            grad_k = transposed_times(grad_scores, q)
            grad_q = grad_q * cos - pltpu.roll(grad_q, HD // 2, 1) * sin
            grad_k = grad_k * cos - pltpu.roll(grad_k, HD // 2, 1) * sin
            q_part = grad_q * (sequence_rows(query_ref, s, chunk, half, lanes) * q_inv)
            k_part = grad_k * (sequence_rows(keys_ref, s, chunk, half, lanes) * k_inv)
            gain_ref[0:1, lanes] += jnp.sum(q_part, axis=0, keepdims=True)
            gain_ref[1:2, lanes] += jnp.sum(k_part, axis=0, keepdims=True)
            q_inner += row_sums(q_part * q_gain_ref[:, lanes])
            k_inner += row_sums(k_part * k_gain_ref[:, lanes])
            store_rows(grad_q_ref, s, chunk, half, lanes, grad_q * q_gain_ref[:, lanes])
            store_rows(grad_k_ref, s, chunk, half, lanes, grad_k * k_gain_ref[:, lanes])
        store_blocks(inner_ref, 0, blocks, q_inner)
        store_blocks(inner_ref, 1, blocks, k_inner)


def attend_back(
    grad_attended, q_rot, k_rot, values, query, keys, squares, q_gain, k_gain, tables, model_width
):
    rows, width = query.shape
    wide = jax.ShapeDtypeStruct((rows, width), jnp.float32)
    return pl.pallas_call(
        functools.partial(attend_back_kernel, model_width),
        out_shape=(
            jax.ShapeDtypeStruct((rows, width), jnp.bfloat16),
            wide,
            wide,
            jax.ShapeDtypeStruct(squares.shape, jnp.float32),
            jax.ShapeDtypeStruct((2, width), jnp.float32),
        ),
        name="attend_back",
        compiler_params=pltpu.CompilerParams(vmem_limit_bytes=20 * MIB),
        cost_estimate=pl.CostEstimate(
            flops=10 * rows * SEQ * width,
            bytes_accessed=26 * rows * width,
            transcendentals=rows * SEQ * width // HD,
        ),
    )(
        grad_attended,
        q_rot,
        k_rot,
        values,
        query,
        keys,
        squares,
        q_gain[None, :],
        k_gain[None, :],
        *tables,
    )


def finish_kernel(model_width, orders, *refs):
    parts = refs[: len(orders) + 1]
    (
        query_ref,
        keys_ref,
        grad_q_ref,
        grad_k_ref,
        grad_values_ref,
        squares_ref,
        out_ref,
        rest_ref,
        inner_ref,
    ) = refs[len(parts) :]
    _, width = query_ref.shape
    count = squares_ref.shape[0]
    blocks = list(range(count))
    for i, row in enumerate(summed_blocks([part.at[:count] for part in parts], orders)):
        inner_ref[i : i + 1, :] = row
    rest = [part[count:, :] for part in parts]
    while len(rest) > 1:
        rest = [rest[i] + rest[i + 1] for i in range(0, len(rest), 2)]
    rest_ref[...] = rest[0]
    for i, source, target in ((0, query_ref, grad_q_ref), (1, keys_ref, grad_k_ref)):
        inverse = column(
            lax.rsqrt(block_row(squares_ref, i, blocks) / model_width + epsilon), HD
        )
        inner = column(block_row(inner_ref, i, blocks) / model_width, HD)
        for h in range(width // HD):
            lanes = slice(h * HD, (h + 1) * HD)
            normed = source[:, lanes] * inverse
            value = inverse * (target[:, lanes] - normed * inner)
            start = i * width + h * HD
            out_ref[:, start : start + HD] = value.astype(jnp.bfloat16)
    out_ref[:, 2 * width :] = grad_values_ref[...]


def finish(query, keys, grad_q, grad_k, grad_values, squares, inner, orders, model_width):
    rows, width = query.shape
    count, lanes = squares.shape
    return pl.pallas_call(
        functools.partial(finish_kernel, model_width, orders),
        out_shape=(
            jax.ShapeDtypeStruct((rows, 3 * width), jnp.bfloat16),
            jax.ShapeDtypeStruct((inner[0].shape[0] - count, lanes), jnp.float32),
        ),
        scratch_shapes=[pltpu.VMEM((count, lanes), jnp.float32)],
        name="finish",
        compiler_params=pltpu.CompilerParams(vmem_limit_bytes=16 * MIB),
        cost_estimate=pl.CostEstimate(
            flops=10 * rows * width, bytes_accessed=24 * rows * width, transcendentals=0
        ),
    )(*inner, query, keys, grad_q, grad_k, grad_values, squares)


def summed_blocks(refs, orders):
    rows = []
    for i in range(refs[0].shape[0]):
        total = refs[0][i : i + 1, :]
        for order, other in zip(orders, refs[1:]):
            total = total + other[order[i] : order[i] + 1, :]
        rows.append(total)
    return rows


def add_blocks_kernel(orders, *refs):
    own, others, out = refs[0], refs[1:-1], refs[-1]
    count = len(orders[0])
    for i in range(count):
        total = own[i : i + 1, :]
        for order, other in zip(orders, others):
            total = total + other[order[i] : order[i] + 1, :]
        out[i : i + 1, :] = total
    if own.shape[0] > count:
        rest = [own[count:, :]] + [other[count:, :] for other in others]
        while len(rest) > 1:
            rest = [rest[i] + rest[i + 1] for i in range(0, len(rest), 2)]
        out[count:, :] = rest[0]


def add_pieces_kernel(*refs):
    total = refs[0][...]
    for ref in refs[1:-1]:
        total = total + ref[...].astype(jnp.float32)
    refs[-1][...] = total.astype(jnp.bfloat16)


def add_pieces(own, others):
    return pl.pallas_call(
        add_pieces_kernel,
        out_shape=jax.ShapeDtypeStruct(own.shape, jnp.bfloat16),
        name="add_pieces",
        compiler_params=pltpu.CompilerParams(vmem_limit_bytes=4 * MIB),
    )(own, *others)


def add_blocks(own, others, orders):
    return pl.pallas_call(
        functools.partial(add_blocks_kernel, orders),
        out_shape=jax.ShapeDtypeStruct(own.shape, own.dtype),
        name="add_blocks",
        compiler_params=pltpu.CompilerParams(vmem_limit_bytes=4 * MIB),
    )(own, *others)


def joined(refs):
    return refs[0][...] if len(refs) == 1 else jnp.concatenate([r[...] for r in refs], axis=0)


def project_kernel(pieces, *refs):
    rows = joined(refs[:pieces])
    w_query_ref, w_key_ref, w_value_ref, query_ref, keys_ref, values_ref, squares_ref = refs[
        pieces:
    ]
    blocks = list(range(squares_ref.shape[0]))
    for i, weight, out in ((0, w_query_ref, query_ref), (1, w_key_ref, keys_ref)):
        value = product(rows, weight[...])
        out[...] = value
        square = value * value
        folded = square[:, :HD]
        for h in range(1, value.shape[1] // HD):
            folded = folded + square[:, h * HD : (h + 1) * HD]
        store_blocks(squares_ref, i, blocks, row_sums(folded))
    values_ref[...] = product(rows, w_value_ref[...]).astype(jnp.bfloat16)


def project(rows, w_query, w_key, w_value, tensor_size):
    count = sum(piece.shape[0] for piece in rows)
    depth, width = w_query.shape
    wide = jax.ShapeDtypeStruct((count, width), jnp.float32)
    return pl.pallas_call(
        functools.partial(project_kernel, len(rows)),
        out_shape=(
            wide,
            wide,
            jax.ShapeDtypeStruct((count, width), jnp.bfloat16),
            jax.ShapeDtypeStruct((tensor_size, 2 * count // tensor_size), jnp.float32),
        ),
        name="project",
        compiler_params=pltpu.CompilerParams(vmem_limit_bytes=20 * MIB),
        cost_estimate=pl.CostEstimate(
            flops=6 * count * depth * width,
            bytes_accessed=2 * count * depth + 6 * depth * width + 10 * count * width,
            transcendentals=0,
        ),
    )(*rows, w_query, w_key, w_value)


def ffn_kernel(pieces, *refs):
    rows = joined(refs[:pieces])
    w_gate_ref, w_up_ref, gate_ref, up_ref, swiglu_ref = refs[pieces:]
    gate = product(rows, w_gate_ref[...])
    up = product(rows, w_up_ref[...])
    gate_ref[...] = gate
    up_ref[...] = up
    swiglu_ref[...] = (gate * jax.nn.sigmoid(gate) * up).astype(jnp.bfloat16)


def ffn(rows, w_gate, w_up):
    count = sum(piece.shape[0] for piece in rows)
    depth, units = w_gate.shape
    tile = min(256, units)
    weight = pl.BlockSpec((depth, tile), lambda j: (0, j))
    out = pl.BlockSpec((count, tile), lambda j: (0, j))
    wide = jax.ShapeDtypeStruct((count, units), jnp.float32)
    return pl.pallas_call(
        functools.partial(ffn_kernel, len(rows)),
        grid=(units // tile,),
        in_specs=[pl.BlockSpec(piece.shape, lambda j: (0, 0)) for piece in rows]
        + [weight, weight],
        out_specs=(out, out, out),
        out_shape=(wide, wide, jax.ShapeDtypeStruct((count, units), jnp.bfloat16)),
        name="ffn",
        compiler_params=pltpu.CompilerParams(vmem_limit_bytes=20 * MIB),
        cost_estimate=pl.CostEstimate(
            flops=4 * count * depth * units,
            bytes_accessed=2 * count * depth + 4 * depth * units + 10 * count * units,
            transcendentals=count * units,
        ),
    )(*rows, w_gate, w_up)


def ffn_back_kernel(pieces, *refs):
    grad = joined(refs[:pieces])
    w_down_ref, gate_ref, up_ref, grad_gate_ref, grad_up_ref = refs[pieces:]
    grad_swiglu = times_transposed(grad, w_down_ref[...])
    gate = gate_ref[...]
    sig = jax.nn.sigmoid(gate)
    grad_gate = grad_swiglu * up_ref[...] * sig * (1.0 + gate * (1.0 - sig))
    grad_gate_ref[...] = grad_gate.astype(jnp.bfloat16)
    grad_up_ref[...] = (grad_swiglu * (gate * sig)).astype(jnp.bfloat16)


def ffn_back(grad, w_down, gate, up):
    count = sum(piece.shape[0] for piece in grad)
    units, depth = w_down.shape
    tile = min(256, units)
    out = pl.BlockSpec((count, tile), lambda j: (0, j))
    narrow = jax.ShapeDtypeStruct((count, units), jnp.bfloat16)
    return pl.pallas_call(
        functools.partial(ffn_back_kernel, len(grad)),
        grid=(units // tile,),
        in_specs=[pl.BlockSpec(piece.shape, lambda j: (0, 0)) for piece in grad]
        + [pl.BlockSpec((tile, depth), lambda j: (j, 0)), out, out],
        out_specs=(out, out),
        out_shape=(narrow, narrow),
        name="ffn_back",
        compiler_params=pltpu.CompilerParams(vmem_limit_bytes=20 * MIB),
        cost_estimate=pl.CostEstimate(
            flops=2 * count * depth * units,
            bytes_accessed=2 * count * depth + 2 * depth * units + 12 * count * units,
            transcendentals=count * units,
        ),
    )(*grad, w_down, gate, up)


def weight_grad_kernel(left_counts, right_counts, rights, outs, *refs):
    groups = len(left_counts)
    left, at = [], 0
    for count in left_counts:
        left.append(joined(refs[at : at + count]))
        at += count
    out_refs = refs[len(refs) - rights * outs :]
    for r in range(rights):
        right = []
        for count in right_counts:
            right.append(refs[at : at + count])
            at += count
        width = right[0][0].shape[1] // outs
        for o in range(outs):
            sums = []
            for g in range(groups):
                pieces = [ref[:, o * width : (o + 1) * width] for ref in right[g]]
                whole = pieces[0] if len(pieces) == 1 else jnp.concatenate(pieces, axis=0)
                sums.append(transposed_times(left[g], whole))
            while len(sums) > 1:
                sums = [sums[i] - sums[i + 1] * -1.0 for i in range(0, len(sums), 2)]
            out_refs[r * outs + o][...] = sums[0]


def weight_grad(left, *rights, outs=1):
    depth = left[0][0].shape[1]
    tile = min(256, depth)
    left_pieces = [piece for group in left for piece in group]
    right_pieces = [piece for right in rights for group in right for piece in group]
    rows = sum(piece.shape[0] for piece in left_pieces)
    widths = [right[0][0].shape[1] // outs for right in rights for _ in range(outs)]
    return pl.pallas_call(
        functools.partial(
            weight_grad_kernel,
            [len(group) for group in left],
            [len(group) for group in rights[0]],
            len(rights),
            outs,
        ),
        grid=(depth // tile,),
        in_specs=[pl.BlockSpec((piece.shape[0], tile), lambda i: (0, i)) for piece in left_pieces]
        + [pl.BlockSpec(piece.shape, lambda i: (0, 0)) for piece in right_pieces],
        out_specs=[pl.BlockSpec((tile, width), lambda i: (i, 0)) for width in widths],
        out_shape=[jax.ShapeDtypeStruct((depth, width), jnp.float32) for width in widths],
        name="weight_grad",
        compiler_params=pltpu.CompilerParams(vmem_limit_bytes=44 * MIB),
        cost_estimate=pl.CostEstimate(
            flops=2 * rows * depth * sum(widths),
            bytes_accessed=2 * rows * (depth + sum(widths)) + 4 * depth * sum(widths),
            transcendentals=0,
        ),
    )(*left_pieces, *right_pieces)


def build(dp_size, tensor_size):
    pairs = tensor_size // 2

    def swap(value, axis, mask):
        size = dp_size if axis == "dp" else tensor_size
        return lax.ppermute(value, axis, [(i, i ^ mask) for i in range(size)])

    def tensor_gather(own):
        near = [own] + [swap(own, "tensor", 2 * k) for k in range(1, pairs)]
        return near + [swap(near[k], "tensor", 1) for k in range(pairs)]

    def tensor_scatter(partial_of, rows):
        half = rows // 2
        far = partial_of(half, rows).astype(jnp.bfloat16)
        far = swap(far, "tensor", 1)
        near = partial_of(0, half) + far.astype(jnp.float32)
        count = half // pairs
        total = near[:count]
        for k in range(1, pairs):
            block = near[k * count : (k + 1) * count].astype(jnp.bfloat16)
            total = total + swap(block, "tensor", 2 * k).astype(jnp.float32)
        return total

    def row_sum(value):
        def order(mask):
            out = []
            for i in range(tensor_size):
                wanted = (2 * (i % pairs) + i // pairs) ^ mask
                out.append((wanted % 2) * pairs + wanted // 2)
            return out

        value = add_blocks(value, [swap(value, "tensor", 1)], [order(1)])
        others = [swap(value, "tensor", 2 * k) for k in range(1, pairs)]
        return [value] + others, [order(2 * k) for k in range(1, pairs)]

    def tree_sum(values):
        while len(values) > 1:
            values = [values[i] + values[i + 1] for i in range(0, len(values), 2)]
        return values[0]

    def dp_gather(own):
        return [[own]] + [[swap(own, "dp", j)] for j in range(1, dp_size)]

    def dp_gather_shared(pieces):
        near = jnp.concatenate(pieces[:pairs], axis=0)
        groups = [[near] + pieces[pairs:]]
        for j in range(1, dp_size):
            piece = swap(near, "dp", j)
            groups.append([piece, swap(piece, "tensor", 1)])
        return groups

    def dp_sum(matrix):
        rows = matrix.shape[0] // dp_size
        rounded = matrix.astype(jnp.bfloat16)
        me = lax.axis_index("dp")
        zero = jnp.zeros_like(me)
        own = lax.dynamic_slice_in_dim(matrix, me * rows, rows, 0)
        others = []
        for j in range(1, dp_size):
            piece = lax.dynamic_slice_in_dim(rounded, (me ^ j) * rows, rows, 0)
            others.append(swap(piece, "dp", j))
        total = add_pieces(own, others)
        result = jnp.zeros(matrix.shape, jnp.float32)
        for j in range(dp_size):
            piece = total if j == 0 else swap(total, "dp", j)
            result = lax.dynamic_update_slice(
                result, piece.astype(jnp.float32), ((me ^ j) * rows, zero)
            )
        return result

    def positions(rows):
        count = rows // tensor_size
        index = jnp.arange(rows, dtype=jnp.int32)
        block = index // count
        mask = 2 * (block % pairs) + block // pairs
        owner = lax.axis_index("tensor").astype(jnp.int32) ^ mask
        return (owner * count + index % count) % SEQ

    def tables_of(rows):
        pos = positions(rows)
        half_width = HD // 2
        exponent = jnp.arange(half_width, dtype=jnp.float32) * (2.0 / HD)
        frequency = rope_base ** (-exponent)
        angles = pos.astype(jnp.float32)[:, None] * frequency[None, :]
        cos, sin = jnp.cos(angles), jnp.sin(angles)
        return (
            jnp.concatenate([cos, cos], axis=1),
            jnp.concatenate([-sin, sin], axis=1),
            pos[None, :],
        )

    def shards(
        tokens,
        cotangent,
        w_query,
        w_key,
        w_value,
        w_out,
        w_gate,
        w_up,
        w_down,
        q_gain,
        k_gain,
        attn_gain,
        ffn_gain,
    ):
        model_width = tokens.shape[1]
        rows = tokens.shape[0] * tensor_size
        width = w_query.shape[1]
        tables = tables_of(rows)

        gathered = tensor_gather(tokens)
        query, keys, values, squares = project(gathered, w_query, w_key, w_value, tensor_size)
        square_parts, orders = row_sum(squares)
        attended, q_rot, k_rot, squares = attend(
            query, keys, values, square_parts, orders, q_gain, k_gain, tables, model_width
        )
        attn_rows = tensor_scatter(lambda a, b: product(attended[a:b], w_out), rows)
        a_inverse = row_scale(attn_rows)
        a_normed = attn_rows * a_inverse
        mixed = tokens.astype(jnp.float32) + a_normed * attn_gain
        mixed_b = tensor_gather(mixed.astype(jnp.bfloat16))
        gate, up_proj, swiglu = ffn(mixed_b, w_gate, w_up)
        ffn_rows = tensor_scatter(lambda a, b: product(swiglu[a:b], w_down), rows)
        m_inverse = row_scale(ffn_rows)
        m_normed = ffn_rows * m_inverse
        layer_out = mixed + m_normed * ffn_gain
        grad_out = cotangent.astype(jnp.float32)
        ffn_gain_part = jnp.sum(grad_out * m_normed, axis=0)
        grad_ffn = tensor_gather(
            norm_back(grad_out * ffn_gain, m_normed, m_inverse).astype(jnp.bfloat16)
        )
        grad_gate, grad_up = ffn_back(grad_ffn, w_down, gate, up_proj)
        grad_mixed = grad_out + tensor_scatter(
            lambda a, b: times_transposed(grad_gate[a:b], w_gate)
            + times_transposed(grad_up[a:b], w_up),
            rows,
        )
        attn_gain_part = jnp.sum(grad_mixed * a_normed, axis=0)
        grad_attn = jnp.concatenate(tensor_gather(
            norm_back(grad_mixed * attn_gain, a_normed, a_inverse).astype(jnp.bfloat16)
        ), axis=0)
        grad_attended = times_transposed(grad_attn, w_out).astype(jnp.bfloat16)
        grad_values, grad_q, grad_k, inner, gain_parts = attend_back(
            grad_attended,
            q_rot,
            k_rot,
            values,
            query,
            keys,
            squares,
            q_gain,
            k_gain,
            tables,
            model_width,
        )
        lanes = inner.shape[1]
        inner_parts, orders = row_sum(
            jnp.concatenate(
                [inner, attn_gain_part.reshape(-1, lanes), ffn_gain_part.reshape(-1, lanes)]
            ),
        )
        grad_qkv, post_gains = finish(
            query, keys, grad_q, grad_k, grad_values, squares, inner_parts, orders, model_width
        )
        grad_tokens = grad_mixed + tensor_scatter(
            lambda a, b: times_transposed(grad_qkv[a:b, :width], w_query)
            + times_transposed(grad_qkv[a:b, width : 2 * width], w_key)
            + times_transposed(grad_qkv[a:b, 2 * width :], w_value),
            rows,
        )

        tokens_all = dp_gather_shared(gathered)
        mixed_all = dp_gather_shared(mixed_b)
        grad_ffn_all = dp_gather_shared(grad_ffn)
        swiglus, grad_gates, grad_ups = [[swiglu]], [[grad_gate]], [[grad_up]]
        for j in range(1, dp_size):
            gate_j, up_j, swiglu_j = ffn(mixed_all[j], w_gate, w_up)
            grad_gate_j, grad_up_j = ffn_back(grad_ffn_all[j], w_down, gate_j, up_j)
            swiglus.append([swiglu_j])
            grad_gates.append([grad_gate_j])
            grad_ups.append([grad_up_j])
        (grad_w_down,) = weight_grad(swiglus, grad_ffn_all)
        grad_w_gate, grad_w_up = weight_grad(mixed_all, grad_gates, grad_ups)
        grad_w_out = dp_sum(transposed_times(attended, grad_attn))
        grad_w_query, grad_w_key, grad_w_value = weight_grad(
            tokens_all, dp_gather(grad_qkv), outs=3
        )
        own_gains = jnp.concatenate([post_gains.reshape(-1), gain_parts.reshape(-1)])
        gains = tree_sum([piece for group in dp_gather(own_gains) for piece in group])
        return (
            layer_out,
            grad_tokens,
            grad_w_query,
            grad_w_key,
            grad_w_value,
            grad_w_out,
            grad_w_gate,
            grad_w_up,
            grad_w_down,
            gains[2 * model_width : 2 * model_width + width],
            gains[2 * model_width + width :],
            gains[:model_width],
            gains[model_width : 2 * model_width],
        )

    return shards


def solution(mesh):
    placed = (
        P(("dp", "tensor"), None),
        P(("dp", "tensor"), None),
        P(None, "tensor"),
        P(None, "tensor"),
        P(None, "tensor"),
        P("tensor", None),
        P(None, "tensor"),
        P(None, "tensor"),
        P("tensor", None),
        P("tensor"),
        P("tensor"),
        P(),
        P(),
    )
    return jax.shard_map(
        build(mesh.shape["dp"], mesh.shape["tensor"]),
        mesh=mesh,
        in_specs=placed,
        out_specs=(
            P(("dp", "tensor"), None),
            P(("dp", "tensor"), None),
            P(None, "tensor"),
            P(None, "tensor"),
            P(None, "tensor"),
            P("tensor", None),
            P(None, "tensor"),
            P(None, "tensor"),
            P("tensor", None),
            P("tensor"),
            P("tensor"),
            P(),
            P(),
        ),
        check_vma=False,
    )
```

```python
import functools
import math

import jax
import jax.numpy as jnp
from jax import lax
from jax.experimental import pallas as pl
from jax.experimental.pallas import tpu as pltpu
from jax.sharding import PartitionSpec as P

HD = 128
SEQ = 256

epsilon = 1e-06
rope_base = 500000.0

MIB = 1 << 20


def row_scale(matrix):
    return lax.rsqrt(jnp.mean(matrix * matrix, axis=1, keepdims=True) + epsilon)


def norm_back(grad_normed, normed, inverse):
    return inverse * (grad_normed - normed * jnp.mean(grad_normed * normed, axis=1, keepdims=True))


def product(left, right):
    return jnp.dot(left, right, preferred_element_type=jnp.float32)


def times_transposed(left, right):
    return lax.dot_general(
        left, right, (((1,), (1,)), ((), ())), preferred_element_type=jnp.float32
    )


def transposed_times(left, right):
    return lax.dot_general(
        left, right, (((0,), (0,)), ((), ())), preferred_element_type=jnp.float32
    )


def column(row, width):
    return jnp.broadcast_to(row, (width, row.shape[1])).T


def row_sums(matrix):
    return jnp.sum(matrix.T, axis=0, keepdims=True)


def sequence_rows(ref, s, chunk, half, lanes):
    top = ref[s * chunk : (s + 1) * chunk, lanes]
    bottom = ref[half + s * chunk : half + (s + 1) * chunk, lanes]
    return jnp.concatenate([top, bottom], axis=0)


def store_rows(ref, s, chunk, half, lanes, value):
    ref[s * chunk : (s + 1) * chunk, lanes] = value[:chunk]
    ref[half + s * chunk : half + (s + 1) * chunk, lanes] = value[chunk:]


def block_row(ref, i, blocks, count):
    return jnp.concatenate(
        [ref[b : b + 1, i * count : (i + 1) * count] for b in blocks], axis=1
    )


def sequence_blocks(ref, s, chunk, count):
    steps = chunk // count
    pairs = ref.shape[0] // 2
    return [h * pairs + s * steps + k for h in range(2) for k in range(steps)]


def store_blocks(ref, i, blocks, row, count):
    for j, b in enumerate(blocks):
        ref[b : b + 1, i * count : (i + 1) * count] = row[:, j * count : (j + 1) * count]


def inverse_column(squares_ref, i, blocks, count, model_width):
    squares = block_row(squares_ref, i, blocks, count)
    return column(lax.rsqrt(squares / model_width + epsilon), HD)


def causal_mask(pos_ref, s, chunk, half):
    key_pos = jnp.concatenate(
        [
            pos_ref[:, s * chunk : (s + 1) * chunk],
            pos_ref[:, half + s * chunk : half + (s + 1) * chunk],
        ],
        axis=1,
    )
    length = 2 * chunk
    key_all = jnp.broadcast_to(key_pos, (length, length))
    return key_all.T >= key_all


def attend_kernel(model_width, orders, *refs):
    parts = refs[: len(orders) + 1]
    (
        query_ref,
        keys_ref,
        values_ref,
        q_gain_ref,
        k_gain_ref,
        cos_ref,
        sin_ref,
        pos_ref,
        attended_ref,
        q_rot_ref,
        k_rot_ref,
        squares_ref,
    ) = refs[len(parts) :]
    for i, row in enumerate(summed_blocks(parts, orders)):
        squares_ref[i : i + 1, :] = row
    rows, width = query_ref.shape
    half = rows // 2
    chunk = SEQ // 2
    for s in range(rows // SEQ):
        every = slice(None)
        cos = sequence_rows(cos_ref, s, chunk, half, every)
        sin = sequence_rows(sin_ref, s, chunk, half, every)
        mask = causal_mask(pos_ref, s, chunk, half)
        count = rows // squares_ref.shape[0]
        blocks = sequence_blocks(squares_ref, s, chunk, count)
        q_inv = inverse_column(squares_ref, 0, blocks, count, model_width)
        k_inv = inverse_column(squares_ref, 1, blocks, count, model_width)

        @pl.loop(0, width // HD)
        def _(h):
            lanes = pl.ds(pl.multiple_of(h * HD, HD), HD)
            q = sequence_rows(query_ref, s, chunk, half, lanes) * q_inv * q_gain_ref[:, lanes]
            k = sequence_rows(keys_ref, s, chunk, half, lanes) * k_inv * k_gain_ref[:, lanes]
            q = (q * cos + pltpu.roll(q, HD // 2, 1) * sin).astype(jnp.bfloat16)
            k = (k * cos + pltpu.roll(k, HD // 2, 1) * sin).astype(jnp.bfloat16)
            store_rows(q_rot_ref, s, chunk, half, lanes, q)
            store_rows(k_rot_ref, s, chunk, half, lanes, k)
            scores = times_transposed(q, k) * (1.0 / math.sqrt(HD))
            scores = jnp.where(mask, scores, -1e30)
            shifted = jnp.exp(scores - jnp.max(scores, axis=1, keepdims=True))
            probs = (shifted / jnp.sum(shifted, axis=1, keepdims=True)).astype(jnp.bfloat16)
            v = sequence_rows(values_ref, s, chunk, half, lanes)
            store_rows(
                attended_ref, s, chunk, half, lanes, product(probs, v).astype(jnp.bfloat16)
            )


def attend(query, keys, values, squares, orders, q_gain, k_gain, tables, model_width):
    rows, width = query.shape
    out = jax.ShapeDtypeStruct((rows, width), jnp.bfloat16)
    return pl.pallas_call(
        functools.partial(attend_kernel, model_width, orders),
        out_shape=(
            out,
            out,
            out,
            jax.ShapeDtypeStruct(squares[0].shape, jnp.float32),
        ),
        name="attend",
        compiler_params=pltpu.CompilerParams(vmem_limit_bytes=16 * MIB),
        cost_estimate=pl.CostEstimate(
            flops=4 * rows * SEQ * width,
            bytes_accessed=16 * rows * width,
            transcendentals=rows * SEQ * width // HD,
        ),
    )(*squares, query, keys, values, q_gain[None, :], k_gain[None, :], *tables)


def attend_back_kernel(model_width, pieces, *refs):
    (
        w_out_ref,
        q_rot_ref,
        k_rot_ref,
        values_ref,
        query_ref,
        keys_ref,
        squares_ref,
        q_gain_ref,
        k_gain_ref,
        cos_ref,
        sin_ref,
        pos_ref,
        grad_values_ref,
        grad_q_ref,
        grad_k_ref,
        inner_ref,
        gain_ref,
        grad_ref,
    ) = refs[pieces:]
    rows, width = query_ref.shape
    grad = times_transposed(joined(refs[:pieces]), w_out_ref[...])
    grad_ref[...] = grad.astype(jnp.bfloat16)
    inner_ref[...] = jnp.zeros_like(inner_ref)
    half = rows // 2
    chunk = SEQ // 2
    scale = 1.0 / math.sqrt(HD)
    gain_ref[...] = jnp.zeros_like(gain_ref)
    for s in range(rows // SEQ):
        every = slice(None)
        cos = sequence_rows(cos_ref, s, chunk, half, every)
        sin = sequence_rows(sin_ref, s, chunk, half, every)
        mask = causal_mask(pos_ref, s, chunk, half)
        count = rows // squares_ref.shape[0]
        blocks = sequence_blocks(squares_ref, s, chunk, count)
        q_inv = inverse_column(squares_ref, 0, blocks, count, model_width)
        k_inv = inverse_column(squares_ref, 1, blocks, count, model_width)

        def head(h, inners):
            q_inner, k_inner = inners
            lanes = pl.ds(pl.multiple_of(h * HD, HD), HD)
            q = sequence_rows(q_rot_ref, s, chunk, half, lanes)
            k = sequence_rows(k_rot_ref, s, chunk, half, lanes)
            v = sequence_rows(values_ref, s, chunk, half, lanes)
            g = sequence_rows(grad_ref, s, chunk, half, lanes)
            scores = times_transposed(q, k) * scale
            scores = jnp.where(mask, scores, -1e30)
            shifted = jnp.exp(scores - jnp.max(scores, axis=1, keepdims=True))
            probs = shifted / jnp.sum(shifted, axis=1, keepdims=True)
            grad_v = transposed_times(probs.astype(jnp.bfloat16), g).astype(jnp.bfloat16)
            store_rows(grad_values_ref, s, chunk, half, lanes, grad_v)
            grad_probs = times_transposed(g, v)
            inner = jnp.sum(probs * grad_probs, axis=1, keepdims=True)
            grad_scores = (probs * (grad_probs - inner) * scale).astype(jnp.bfloat16)
            grad_q = product(grad_scores, k)
            grad_k = transposed_times(grad_scores, q)
            grad_q = grad_q * cos - pltpu.roll(grad_q, HD // 2, 1) * sin
            grad_k = grad_k * cos - pltpu.roll(grad_k, HD // 2, 1) * sin
            q_part = grad_q * (sequence_rows(query_ref, s, chunk, half, lanes) * q_inv)
            k_part = grad_k * (sequence_rows(keys_ref, s, chunk, half, lanes) * k_inv)
            gain_ref[0:1, lanes] += jnp.sum(q_part, axis=0, keepdims=True)
            gain_ref[1:2, lanes] += jnp.sum(k_part, axis=0, keepdims=True)
            q_inner = q_inner + row_sums(q_part * q_gain_ref[:, lanes])
            k_inner = k_inner + row_sums(k_part * k_gain_ref[:, lanes])
            store_rows(grad_q_ref, s, chunk, half, lanes, grad_q * q_gain_ref[:, lanes])
            store_rows(grad_k_ref, s, chunk, half, lanes, grad_k * k_gain_ref[:, lanes])
            return q_inner, k_inner

        zero = jnp.zeros((1, SEQ), jnp.float32)
        q_inner, k_inner = lax.fori_loop(0, width // HD, head, (zero, zero))
        store_blocks(inner_ref, 0, blocks, q_inner, count)
        store_blocks(inner_ref, 1, blocks, k_inner, count)


def attend_back(
    grad_attn, w_out, q_rot, k_rot, values, query, keys, squares, q_gain, k_gain, tables, model_width
):
    rows, width = query.shape
    wide = jax.ShapeDtypeStruct((rows, width), jnp.float32)
    return pl.pallas_call(
        functools.partial(attend_back_kernel, model_width, len(grad_attn)),
        out_shape=(
            jax.ShapeDtypeStruct((rows, width), jnp.bfloat16),
            wide,
            wide,
            jax.ShapeDtypeStruct(squares.shape, jnp.float32),
            jax.ShapeDtypeStruct((2, width), jnp.float32),
        ),
        scratch_shapes=[pltpu.VMEM((rows, width), jnp.bfloat16)],
        name="attend_back",
        compiler_params=pltpu.CompilerParams(vmem_limit_bytes=16 * MIB),
        cost_estimate=pl.CostEstimate(
            flops=10 * rows * SEQ * width,
            bytes_accessed=26 * rows * width,
            transcendentals=rows * SEQ * width // HD,
        ),
    )(
        *grad_attn,
        w_out,
        q_rot,
        k_rot,
        values,
        query,
        keys,
        squares,
        q_gain[None, :],
        k_gain[None, :],
        *tables,
    )


def finish_kernel(model_width, orders, *refs):
    parts = refs[: len(orders) + 1]
    (
        query_ref,
        keys_ref,
        grad_q_ref,
        grad_k_ref,
        grad_values_ref,
        squares_ref,
        gains_ref,
        out_ref,
        inner_ref,
        gain_rows_ref,
    ) = refs[len(parts) :]
    rows, width = query_ref.shape
    blocks = list(range(squares_ref.shape[0]))
    count = rows // len(blocks)
    sums = summed_blocks([part.at[: len(blocks)] for part in parts], orders)
    for i, row in enumerate(sums):
        inner_ref[i : i + 1, :] = row
    for i, source, target in ((0, query_ref, grad_q_ref), (1, keys_ref, grad_k_ref)):
        inverse = inverse_column(squares_ref, i, blocks, count, model_width)
        inner = column(block_row(inner_ref, i, blocks, count) / model_width, HD)
        for h in range(width // HD):
            lanes = slice(h * HD, (h + 1) * HD)
            normed = source[:, lanes] * inverse
            value = inverse * (target[:, lanes] - normed * inner)
            start = i * width + h * HD
            out_ref[:rows, start : start + HD] = value.astype(jnp.bfloat16)
    out_ref[:rows, 2 * width :] = grad_values_ref[...]
    rest = [part[len(blocks) :, :] for part in parts]
    while len(rest) > 1:
        rest = [rest[i] + rest[i + 1] for i in range(0, len(rest), 2)]
    rest = rest[0]
    gains = [rest[i : i + 1, :] for i in range(rest.shape[0])]
    for i in range(2):
        gains += [gains_ref[i : i + 1, h * HD : (h + 1) * HD] for h in range(width // HD)]
    gain_rows_ref[...] = jnp.zeros_like(gain_rows_ref)
    across = 3 * width // HD
    half = gain_rows_ref.shape[0] // 2
    for i, gain in enumerate(gains):
        r, lanes = i // across, slice(i % across * HD, (i % across + 1) * HD)
        gain_rows_ref[r : r + 1, lanes] = gain
    high = gain_rows_ref[:half, :].astype(jnp.bfloat16).astype(jnp.float32)
    gain_rows_ref[half:, :] = gain_rows_ref[:half, :] - high
    out_ref[rows:, :] = gain_rows_ref[...].astype(jnp.bfloat16)


def gain_row_count(model_width, width):
    blocks = (2 * model_width + 2 * width) // HD
    return 16 * pl.cdiv(pl.cdiv(blocks, 3 * width // HD), 8)


def finish(query, keys, grad_q, grad_k, grad_values, squares, inner, gains, orders, model_width):
    rows, width = query.shape
    extra = gain_row_count(model_width, width)
    return pl.pallas_call(
        functools.partial(finish_kernel, model_width, orders),
        out_shape=jax.ShapeDtypeStruct((rows + extra, 3 * width), jnp.bfloat16),
        scratch_shapes=[
            pltpu.VMEM(squares.shape, jnp.float32),
            pltpu.VMEM((extra, 3 * width), jnp.float32),
        ],
        name="finish",
        compiler_params=pltpu.CompilerParams(vmem_limit_bytes=16 * MIB),
        cost_estimate=pl.CostEstimate(
            flops=10 * rows * width, bytes_accessed=24 * rows * width, transcendentals=0
        ),
    )(*inner, query, keys, grad_q, grad_k, grad_values, squares, gains)


def sum_gains_kernel(*refs):
    groups = refs[:-4]
    half = groups[0].shape[0] // 2
    values = []
    for ref in groups:
        values.append(ref[:half, :].astype(jnp.float32) + ref[half:, :].astype(jnp.float32))
    while len(values) > 1:
        values = [values[i] + values[i + 1] for i in range(0, len(values), 2)]
    total = values[0]
    across = total.shape[1] // HD
    at = 0
    for out in refs[-4:]:
        for j in range(out.shape[1] // HD):
            r, c = at // across, at % across
            out[:, j * HD : (j + 1) * HD] = total[r : r + 1, c * HD : (c + 1) * HD]
            at += 1


def sum_gains(groups, model_width, width):
    extra = gain_row_count(model_width, width)
    at = [group.shape[0] // extra - 1 for group in groups]
    shapes = [(1, model_width), (1, model_width), (1, width), (1, width)]
    outs = pl.pallas_call(
        sum_gains_kernel,
        grid=(1,),
        in_specs=[pl.BlockSpec((extra, 3 * width), lambda i, j=j: (j, 0)) for j in at],
        out_specs=[pl.BlockSpec(shape, lambda i: (0, 0)) for shape in shapes],
        out_shape=[jax.ShapeDtypeStruct(shape, jnp.float32) for shape in shapes],
        name="sum_gains",
        compiler_params=pltpu.CompilerParams(vmem_limit_bytes=4 * MIB),
    )(*groups)
    return [out[0] for out in outs]


def back_product(grad_ref, weights):
    width = weights[0].shape[1]
    return sum(
        times_transposed(grad_ref[:, i * width : (i + 1) * width], weight[...])
        for i, weight in enumerate(weights)
    )


def far_kernel(grad_ref, *refs):
    refs[-1][...] = back_product(grad_ref, refs[:-1]).astype(jnp.bfloat16)


def near_kernel(count, grad_ref, far_ref, *refs):
    own_ref, others = refs[3], refs[4:]
    total = back_product(grad_ref, refs[:3]) + far_ref[...].astype(jnp.float32)
    own_ref[...] = total[:count]
    for k, ref in enumerate(others):
        ref[...] = total[(k + 1) * count : (k + 2) * count].astype(jnp.bfloat16)


def tokens_back(grad, weights, half, part, far=None, count=None):
    depth, width = weights[0].shape
    tile = min(512, depth)
    specs = [pl.BlockSpec((half, 3 * width), lambda j: (part, 0))]
    arrays = [grad]
    if far is not None:
        specs.append(pl.BlockSpec((half, tile), lambda j: (0, j)))
        arrays.append(far)
    specs += [pl.BlockSpec((tile, width), lambda j: (j, 0))] * 3
    if far is None:
        kernel, sizes = far_kernel, [(half, jnp.bfloat16)]
    else:
        kernel = functools.partial(near_kernel, count)
        sizes = [(count, jnp.float32)] + [(count, jnp.bfloat16)] * (half // count - 1)
    return pl.pallas_call(
        kernel,
        grid=(depth // tile,),
        in_specs=specs,
        out_specs=[pl.BlockSpec((size, tile), lambda j: (0, j)) for size, _ in sizes],
        out_shape=[jax.ShapeDtypeStruct((size, depth), kind) for size, kind in sizes],
        name="tokens_back",
        compiler_params=pltpu.CompilerParams(vmem_limit_bytes=16 * MIB),
        cost_estimate=pl.CostEstimate(
            flops=6 * half * depth * width,
            bytes_accessed=6 * depth * width + 8 * half * depth,
            transcendentals=0,
        ),
    )(*arrays, *weights)


def out_grad_kernel(pieces, *refs):
    attended_ref, me_ref = refs[pieces : pieces + 2]
    own_ref, others, grad_ref = refs[pieces + 2], refs[pieces + 3 : -1], refs[-1]
    count = own_ref.shape[0]
    grad_ref[...] = transposed_times(attended_ref[...], joined(refs[:pieces]))
    me = me_ref[0]
    own_ref[...] = grad_ref[pl.ds(pl.multiple_of(me * count, count), count), :]
    for j, ref in enumerate(others):
        start = pl.multiple_of((me ^ (j + 1)) * count, count)
        ref[...] = grad_ref[pl.ds(start, count), :].astype(jnp.bfloat16)


def out_grad(attended, grad_attn, me, dp_size):
    width, depth = attended.shape[1], grad_attn[0].shape[1]
    piece = (width // dp_size, depth)
    return pl.pallas_call(
        functools.partial(out_grad_kernel, len(grad_attn)),
        in_specs=[pl.BlockSpec(array.shape, lambda: (0, 0)) for array in (*grad_attn, attended)]
        + [pl.BlockSpec(memory_space=pltpu.SMEM)],
        out_shape=[jax.ShapeDtypeStruct(piece, jnp.float32)]
        + [jax.ShapeDtypeStruct(piece, jnp.bfloat16)] * (dp_size - 1),
        scratch_shapes=[pltpu.VMEM((width, depth), jnp.float32)],
        name="out_grad",
        compiler_params=pltpu.CompilerParams(vmem_limit_bytes=16 * MIB),
        cost_estimate=pl.CostEstimate(
            flops=2 * attended.shape[0] * width * depth,
            bytes_accessed=2 * attended.shape[0] * (width + depth) + 3 * width * depth,
            transcendentals=0,
        ),
    )(*grad_attn, attended, me)


def assemble_kernel(*refs):
    me = refs[-2][0]
    out_ref = refs[-1]
    for j, ref in enumerate(refs[:-2]):
        count = ref.shape[0]
        start = pl.multiple_of((me ^ j) * count, count)
        out_ref[pl.ds(start, count), :] = ref[...].astype(jnp.float32)


def assemble(pieces, me):
    count, depth = pieces[0].shape
    return pl.pallas_call(
        assemble_kernel,
        in_specs=[pl.BlockSpec((count, depth), lambda: (0, 0)) for _ in pieces]
        + [pl.BlockSpec(memory_space=pltpu.SMEM)],
        out_shape=jax.ShapeDtypeStruct((len(pieces) * count, depth), jnp.float32),
        name="assemble",
        compiler_params=pltpu.CompilerParams(vmem_limit_bytes=8 * MIB),
    )(*pieces, me)


def summed_blocks(refs, orders):
    rows = []
    for i in range(refs[0].shape[0]):
        total = refs[0][i : i + 1, :]
        for order, other in zip(orders, refs[1:]):
            total = total + other[order[i] : order[i] + 1, :]
        rows.append(total)
    return rows


def add_blocks_kernel(orders, *refs):
    own, others, out = refs[0], refs[1:-1], refs[-1]
    count = len(orders[0])
    for i in range(count):
        total = own[i : i + 1, :]
        for order, other in zip(orders, others):
            total = total + other[order[i] : order[i] + 1, :]
        out[i : i + 1, :] = total
    if own.shape[0] > count:
        rest = [own[count:, :]] + [other[count:, :] for other in others]
        while len(rest) > 1:
            rest = [rest[i] + rest[i + 1] for i in range(0, len(rest), 2)]
        out[count:, :] = rest[0]


def add_pieces_kernel(*refs):
    total = refs[0][...]
    for ref in refs[1:-1]:
        total = total + ref[...].astype(jnp.float32)
    refs[-1][...] = total.astype(jnp.bfloat16)


def add_pieces(own, others):
    return pl.pallas_call(
        add_pieces_kernel,
        out_shape=jax.ShapeDtypeStruct(own.shape, jnp.bfloat16),
        name="add_pieces",
        compiler_params=pltpu.CompilerParams(vmem_limit_bytes=4 * MIB),
    )(own, *others)


def add_blocks(own, others, orders):
    return pl.pallas_call(
        functools.partial(add_blocks_kernel, orders),
        out_shape=jax.ShapeDtypeStruct(own.shape, own.dtype),
        name="add_blocks",
        compiler_params=pltpu.CompilerParams(vmem_limit_bytes=4 * MIB),
    )(own, *others)


def in_hbm(array):
    return pltpu.with_memory_space_constraint(array, pltpu.HBM)


def resident(shape):
    return pl.BlockSpec(shape, lambda i: (0, 0), pipeline_mode=pl.Buffered(1))


def joined(refs):
    return refs[0][...] if len(refs) == 1 else jnp.concatenate([r[...] for r in refs], axis=0)


def project_kernel(pieces, *refs):
    rows = joined(refs[:pieces])
    w_query_ref, w_key_ref, w_value_ref, query_ref, keys_ref, values_ref, squares_ref = refs[
        pieces:
    ]
    blocks = list(range(squares_ref.shape[0]))
    count = rows.shape[0] // len(blocks)
    if 2 * count < squares_ref.shape[1]:
        squares_ref[...] = jnp.zeros_like(squares_ref)
    for i, weight, out in ((0, w_query_ref, query_ref), (1, w_key_ref, keys_ref)):
        value = product(rows, weight[...])
        out[...] = value
        square = value * value
        folded = square[:, :HD]
        for h in range(1, value.shape[1] // HD):
            folded = folded + square[:, h * HD : (h + 1) * HD]
        store_blocks(squares_ref, i, blocks, row_sums(folded), count)
    values_ref[...] = product(rows, w_value_ref[...]).astype(jnp.bfloat16)


def project(rows, w_query, w_key, w_value, tensor_size):
    count = sum(piece.shape[0] for piece in rows)
    depth, width = w_query.shape
    wide = jax.ShapeDtypeStruct((count, width), jnp.float32)
    return pl.pallas_call(
        functools.partial(project_kernel, len(rows)),
        out_shape=(
            wide,
            wide,
            jax.ShapeDtypeStruct((count, width), jnp.bfloat16),
            jax.ShapeDtypeStruct((tensor_size, max(HD, 2 * count // tensor_size)), jnp.float32),
        ),
        name="project",
        compiler_params=pltpu.CompilerParams(vmem_limit_bytes=16 * MIB),
        cost_estimate=pl.CostEstimate(
            flops=6 * count * depth * width,
            bytes_accessed=2 * count * depth + 6 * depth * width + 10 * count * width,
            transcendentals=0,
        ),
    )(*[in_hbm(array) for array in (*rows, w_query, w_key, w_value)])


def ffn_kernel(pieces, *refs):
    rows = joined(refs[:pieces])
    w_gate_ref, w_up_ref, gate_ref, up_ref, swiglu_ref = refs[pieces:]
    gate = product(rows, w_gate_ref[...])
    up = product(rows, w_up_ref[...])
    gate_ref[...] = gate
    up_ref[...] = up
    swiglu_ref[...] = (gate * jax.nn.sigmoid(gate) * up).astype(jnp.bfloat16)


def ffn(rows, w_gate, w_up):
    count = sum(piece.shape[0] for piece in rows)
    depth, units = w_gate.shape
    tile = min(256, units)
    weight = pl.BlockSpec((depth, tile), lambda j: (0, j))
    out = pl.BlockSpec((count, tile), lambda j: (0, j))
    wide = jax.ShapeDtypeStruct((count, units), jnp.float32)
    return pl.pallas_call(
        functools.partial(ffn_kernel, len(rows)),
        grid=(units // tile,),
        in_specs=[resident(piece.shape) for piece in rows]
        + [weight, weight],
        out_specs=(out, out, out),
        out_shape=(wide, wide, jax.ShapeDtypeStruct((count, units), jnp.bfloat16)),
        name="ffn",
        compiler_params=pltpu.CompilerParams(vmem_limit_bytes=16 * MIB),
        cost_estimate=pl.CostEstimate(
            flops=4 * count * depth * units,
            bytes_accessed=2 * count * depth + 4 * depth * units + 10 * count * units,
            transcendentals=count * units,
        ),
    )(*rows, w_gate, w_up)


def ffn_back_kernel(pieces, *refs):
    grad = joined(refs[:pieces])
    w_down_ref, gate_ref, up_ref, grad_gate_ref, grad_up_ref = refs[pieces:]
    grad_swiglu = times_transposed(grad, w_down_ref[...])
    gate = gate_ref[...]
    sig = jax.nn.sigmoid(gate)
    grad_gate = grad_swiglu * up_ref[...] * sig * (1.0 + gate * (1.0 - sig))
    grad_gate_ref[...] = grad_gate.astype(jnp.bfloat16)
    grad_up_ref[...] = (grad_swiglu * (gate * sig)).astype(jnp.bfloat16)


def ffn_back(grad, w_down, gate, up, place=lambda array: array):
    count = sum(piece.shape[0] for piece in grad)
    units, depth = w_down.shape
    tile = min(256, units)
    out = pl.BlockSpec((count, tile), lambda j: (0, j))
    narrow = jax.ShapeDtypeStruct((count, units), jnp.bfloat16)
    return pl.pallas_call(
        functools.partial(ffn_back_kernel, len(grad)),
        grid=(units // tile,),
        in_specs=[resident(piece.shape) for piece in grad]
        + [pl.BlockSpec((tile, depth), lambda j: (j, 0)), out, out],
        out_specs=(out, out),
        out_shape=(narrow, narrow),
        name="ffn_back",
        compiler_params=pltpu.CompilerParams(vmem_limit_bytes=16 * MIB),
        cost_estimate=pl.CostEstimate(
            flops=2 * count * depth * units,
            bytes_accessed=2 * count * depth + 2 * depth * units + 12 * count * units,
            transcendentals=count * units,
        ),
    )(*grad, *[place(array) for array in (w_down, gate, up)])


def weight_grad_kernel(left_counts, right_counts, rights, outs, *refs):
    groups = len(left_counts)
    left, at = [], 0
    for count in left_counts:
        left.append(joined(refs[at : at + count]))
        at += count
    out_refs = refs[len(refs) - rights * outs :]
    for r in range(rights):
        right = []
        for count in right_counts:
            right.append(refs[at : at + count])
            at += count
        width = right[0][0].shape[1] // outs
        for o in range(outs):
            sums = []
            for g in range(groups):
                pieces = [ref[:, o * width : (o + 1) * width] for ref in right[g]]
                whole = pieces[0] if len(pieces) == 1 else jnp.concatenate(pieces, axis=0)
                sums.append(transposed_times(left[g], whole))
            while len(sums) > 1:
                sums = [sums[i] - sums[i + 1] * -1.0 for i in range(0, len(sums), 2)]
            out_refs[r * outs + o][...] = sums[0]


def weight_grad(left, *rights, outs=1, extra=0):
    depth = left[0][0].shape[1]
    left_pieces = [piece for group in left for piece in group]
    right_pieces, counts = [], []
    for right in rights:
        for group in right:
            right_pieces += group
            counts += [piece.shape[0] for piece in group[:-1]] + [group[-1].shape[0] - extra]
    rows = sum(piece.shape[0] for piece in left_pieces)
    widths = [right[0][0].shape[1] // outs for right in rights for _ in range(outs)]
    tile = min(512 if max(widths) <= 1024 else 256, depth)
    blocks = 4 * rows * tile + (2 * len(rights)) * rows * rights[0][0][0].shape[1]
    needed = blocks + 4 * tile * sum(widths) * (2 + len(left)) + 4 * MIB
    return pl.pallas_call(
        functools.partial(
            weight_grad_kernel,
            [len(group) for group in left],
            [len(group) for group in rights[0]],
            len(rights),
            outs,
        ),
        grid=(depth // tile,),
        in_specs=[pl.BlockSpec((piece.shape[0], tile), lambda i: (0, i)) for piece in left_pieces]
        + [
            resident((count, piece.shape[1])) for count, piece in zip(counts, right_pieces)
        ],
        out_specs=[pl.BlockSpec((tile, width), lambda i: (i, 0)) for width in widths],
        out_shape=[jax.ShapeDtypeStruct((depth, width), jnp.float32) for width in widths],
        name="weight_grad",
        compiler_params=pltpu.CompilerParams(vmem_limit_bytes=max(28 * MIB, needed)),
        cost_estimate=pl.CostEstimate(
            flops=2 * rows * depth * sum(widths),
            bytes_accessed=2 * rows * (depth + sum(widths)) + 4 * depth * sum(widths),
            transcendentals=0,
        ),
    )(*[in_hbm(piece) for piece in left_pieces + right_pieces])


def build(dp_size, tensor_size):
    pairs = tensor_size // 2

    def swap(value, axis, mask):
        size = dp_size if axis == "dp" else tensor_size
        return lax.ppermute(value, axis, [(i, i ^ mask) for i in range(size)])

    def tensor_gather(own, relay=False):
        near = [own]
        for k in range(1, pairs):
            if relay and k == 3:
                near.append(swap(near[2], "tensor", 2))
            else:
                near.append(swap(own, "tensor", 2 * k))
        return near + [swap(near[k], "tensor", 1) for k in range(pairs)]

    def tensor_scatter(partial_of, rows, relay=False):
        half = rows // 2
        far = partial_of(half, rows).astype(jnp.bfloat16)
        far = swap(far, "tensor", 1)
        near = partial_of(0, half) + far.astype(jnp.float32)
        count = half // pairs
        total = near[:count]
        if relay and pairs == 4:
            one, two, three = [near[k * count : (k + 1) * count] for k in range(1, pairs)]
            three = swap(three.astype(jnp.bfloat16), "tensor", 2)
            one = swap(one.astype(jnp.bfloat16), "tensor", 2)
            two = (two + three.astype(jnp.float32)).astype(jnp.bfloat16)
            two = swap(two, "tensor", 4)
            return total + one.astype(jnp.float32) + two.astype(jnp.float32)
        for k in range(1, pairs):
            block = near[k * count : (k + 1) * count].astype(jnp.bfloat16)
            total = total + swap(block, "tensor", 2 * k).astype(jnp.float32)
        return total

    def row_sum(value):
        def order(mask):
            out = []
            for i in range(tensor_size):
                wanted = (2 * (i % pairs) + i // pairs) ^ mask
                out.append((wanted % 2) * pairs + wanted // 2)
            return out

        value = add_blocks(value, [swap(value, "tensor", 1)], [order(1)])
        others = [swap(value, "tensor", 2 * k) for k in range(1, pairs)]
        return [value] + others, [order(2 * k) for k in range(1, pairs)]

    def dp_gather(own, cut):
        if dp_size == 4:
            one = swap(own, "dp", 1)
            two = swap(own, "dp", 2)
            top = one[:cut]
            bottom = two[cut:]
            top = swap(top, "dp", 2)
            bottom = swap(bottom, "dp", 1)
            return [[own], [one], [two], [top, bottom]]
        return [[own]] + [[swap(own, "dp", j)] for j in range(1, dp_size)]

    def dp_gather_shared(pieces):
        near = jnp.concatenate(pieces[:pairs], axis=0)
        fetched = dp_gather(near, near.shape[0] // 2)[1:]
        groups = [[near] + pieces[pairs:]]
        for mine in fetched:
            groups.append(mine + [swap(piece, "tensor", 1) for piece in mine])
        return groups

    def dp_sum(own, others, me):
        others = [swap(piece, "dp", j + 1) for j, piece in enumerate(others)]
        total = add_pieces(own, others)
        pieces = [total] + [swap(total, "dp", j) for j in range(1, dp_size)]
        return assemble(pieces, me)

    def positions(rows):
        count = rows // tensor_size
        index = jnp.arange(rows, dtype=jnp.int32)
        block = index // count
        mask = 2 * (block % pairs) + block // pairs
        owner = lax.axis_index("tensor").astype(jnp.int32) ^ mask
        return (owner * count + index % count) % SEQ

    def tables_of(rows):
        pos = positions(rows)
        half_width = HD // 2
        exponent = jnp.arange(half_width, dtype=jnp.float32) * (2.0 / HD)
        frequency = rope_base ** (-exponent)
        angles = pos.astype(jnp.float32)[:, None] * frequency[None, :]
        cos, sin = jnp.cos(angles), jnp.sin(angles)
        return (
            jnp.concatenate([cos, cos], axis=1),
            jnp.concatenate([-sin, sin], axis=1),
            pos[None, :],
        )

    def shards(
        tokens,
        cotangent,
        w_query,
        w_key,
        w_value,
        w_out,
        w_gate,
        w_up,
        w_down,
        q_gain,
        k_gain,
        attn_gain,
        ffn_gain,
    ):
        model_width = tokens.shape[1]
        rows = tokens.shape[0] * tensor_size
        width = w_query.shape[1]
        tables = tables_of(rows)

        gathered = tensor_gather(tokens, relay=True)
        query, keys, values, squares = project(gathered, w_query, w_key, w_value, tensor_size)
        square_parts, orders = row_sum(squares)
        attended, q_rot, k_rot, squares = attend(
            query, keys, values, square_parts, orders, q_gain, k_gain, tables, model_width
        )
        attn_rows = tensor_scatter(lambda a, b: product(attended[a:b], w_out), rows, relay=True)
        a_inverse = row_scale(attn_rows)
        a_normed = attn_rows * a_inverse
        mixed = tokens.astype(jnp.float32) + a_normed * attn_gain
        mixed_b = tensor_gather(mixed.astype(jnp.bfloat16), relay=True)
        gate, up_proj, swiglu = ffn(mixed_b, w_gate, w_up)
        ffn_rows = tensor_scatter(lambda a, b: product(swiglu[a:b], w_down), rows, relay=True)
        m_inverse = row_scale(ffn_rows)
        m_normed = ffn_rows * m_inverse
        layer_out = mixed + m_normed * ffn_gain
        grad_out = cotangent.astype(jnp.float32)
        ffn_gain_part = jnp.sum(grad_out * m_normed, axis=0)
        grad_ffn = tensor_gather(
            norm_back(grad_out * ffn_gain, m_normed, m_inverse).astype(jnp.bfloat16), relay=True
        )
        grad_gate, grad_up = ffn_back(grad_ffn, w_down, gate, up_proj)
        grad_mixed = grad_out + tensor_scatter(
            lambda a, b: times_transposed(grad_gate[a:b], w_gate)
            + times_transposed(grad_up[a:b], w_up),
            rows,
            relay=True,
        )
        attn_gain_part = jnp.sum(grad_mixed * a_normed, axis=0)
        grad_attn = tensor_gather(
            norm_back(grad_mixed * attn_gain, a_normed, a_inverse).astype(jnp.bfloat16), relay=True
        )
        me = lax.axis_index("dp").astype(jnp.int32).reshape(1)
        grad_values, grad_q, grad_k, inner, gain_parts = attend_back(
            grad_attn,
            w_out,
            q_rot,
            k_rot,
            values,
            query,
            keys,
            squares,
            q_gain,
            k_gain,
            tables,
            model_width,
        )
        lanes = inner.shape[1]
        inner_parts, orders = row_sum(
            jnp.concatenate(
                [inner, attn_gain_part.reshape(-1, lanes), ffn_gain_part.reshape(-1, lanes)]
            ),
        )
        out_own, *out_others = out_grad(attended, grad_attn, me, dp_size)
        grad_qkv = finish(
            query,
            keys,
            grad_q,
            grad_k,
            grad_values,
            squares,
            inner_parts,
            gain_parts,
            orders,
            model_width,
        )
        weights = (w_query, w_key, w_value)
        (far,) = tokens_back(grad_qkv, weights, rows // 2, 1)
        far = swap(far, "tensor", 1)
        own, *others = tokens_back(
            grad_qkv, weights, rows // 2, 0, far, tokens.shape[0]
        )
        others = [swap(piece, "tensor", 2 * k + 2) for k, piece in enumerate(others)]
        grad_tokens = grad_mixed + sum([piece.astype(jnp.float32) for piece in others], own)

        tokens_all = dp_gather_shared(gathered)
        mixed_all = dp_gather_shared(mixed_b)
        grad_ffn_all = dp_gather_shared(grad_ffn)
        swiglus, grad_gates, grad_ups = [[swiglu]], [[grad_gate]], [[grad_up]]
        for j in range(1, dp_size):
            gate_j, up_j, swiglu_j = ffn(mixed_all[j], w_gate, w_up)
            grad_gate_j, grad_up_j = ffn_back(
                grad_ffn_all[j], w_down, gate_j, up_j, *[in_hbm][: j // (dp_size - 1)]
            )
            swiglus.append([swiglu_j])
            grad_gates.append([grad_gate_j])
            grad_ups.append([grad_up_j])
        (grad_w_down,) = weight_grad(swiglus, grad_ffn_all)
        (grad_w_gate,) = weight_grad(mixed_all, grad_gates)
        (grad_w_up,) = weight_grad(mixed_all, grad_ups)
        grad_w_out = dp_sum(out_own, out_others, me)
        operands = dp_gather(grad_qkv, rows // 2)
        grad_w_query, grad_w_key, grad_w_value = weight_grad(
            tokens_all, operands, outs=3, extra=grad_qkv.shape[0] - rows
        )
        gains = sum_gains([group[-1] for group in operands], model_width, width)
        return (
            layer_out,
            grad_tokens,
            grad_w_query,
            grad_w_key,
            grad_w_value,
            grad_w_out,
            grad_w_gate,
            grad_w_up,
            grad_w_down,
            gains[2],
            gains[3],
            gains[0],
            gains[1],
        )

    return shards


def solution(mesh):
    placed = (
        P(("dp", "tensor"), None),
        P(("dp", "tensor"), None),
        P(None, "tensor"),
        P(None, "tensor"),
        P(None, "tensor"),
        P("tensor", None),
        P(None, "tensor"),
        P(None, "tensor"),
        P("tensor", None),
        P("tensor"),
        P("tensor"),
        P(),
        P(),
    )
    return jax.shard_map(
        build(mesh.shape["dp"], mesh.shape["tensor"]),
        mesh=mesh,
        in_specs=placed,
        out_specs=(
            P(("dp", "tensor"), None),
            P(("dp", "tensor"), None),
            P(None, "tensor"),
            P(None, "tensor"),
            P(None, "tensor"),
            P("tensor", None),
            P(None, "tensor"),
            P(None, "tensor"),
            P("tensor", None),
            P("tensor"),
            P("tensor"),
            P(),
            P(),
        ),
        check_vma=False,
    )
```

```python
import functools
import math

import jax
import jax.numpy as jnp
from jax import lax
from jax.experimental import pallas as pl
from jax.experimental.pallas import tpu as pltpu
from jax.sharding import PartitionSpec as P

HD = 128
SEQ = 256

epsilon = 1e-06
rope_base = 500000.0

MIB = 1 << 20


def row_scale(matrix):
    return lax.rsqrt(jnp.mean(matrix * matrix, axis=1, keepdims=True) + epsilon)


def norm_back(grad_normed, normed, inverse):
    return inverse * (grad_normed - normed * jnp.mean(grad_normed * normed, axis=1, keepdims=True))


def product(left, right):
    return jnp.dot(left, right, preferred_element_type=jnp.float32)


def times_transposed(left, right):
    return lax.dot_general(
        left, right, (((1,), (1,)), ((), ())), preferred_element_type=jnp.float32
    )


def transposed_times(left, right):
    return lax.dot_general(
        left, right, (((0,), (0,)), ((), ())), preferred_element_type=jnp.float32
    )


def column(row, width):
    return jnp.broadcast_to(row, (width, row.shape[1])).T


def row_sums(matrix):
    return jnp.sum(matrix.T, axis=0, keepdims=True)


def sequence_rows(ref, s, chunk, half, lanes):
    top = ref[s * chunk : (s + 1) * chunk, lanes]
    bottom = ref[half + s * chunk : half + (s + 1) * chunk, lanes]
    return jnp.concatenate([top, bottom], axis=0)


def store_rows(ref, s, chunk, half, lanes, value):
    ref[s * chunk : (s + 1) * chunk, lanes] = value[:chunk]
    ref[half + s * chunk : half + (s + 1) * chunk, lanes] = value[chunk:]


def block_row(ref, i, blocks, count):
    return jnp.concatenate(
        [ref[b : b + 1, i * count : (i + 1) * count] for b in blocks], axis=1
    )


def sequence_blocks(ref, s, chunk, count):
    steps = chunk // count
    pairs = ref.shape[0] // 2
    return [h * pairs + s * steps + k for h in range(2) for k in range(steps)]


def store_blocks(ref, i, blocks, row, count):
    for j, b in enumerate(blocks):
        ref[b : b + 1, i * count : (i + 1) * count] = row[:, j * count : (j + 1) * count]


def inverse_column(squares_ref, i, blocks, count, model_width):
    squares = block_row(squares_ref, i, blocks, count)
    return column(lax.rsqrt(squares / model_width + epsilon), HD)


def causal_mask(pos_ref, s, chunk, half):
    key_pos = jnp.concatenate(
        [
            pos_ref[:, s * chunk : (s + 1) * chunk],
            pos_ref[:, half + s * chunk : half + (s + 1) * chunk],
        ],
        axis=1,
    )
    length = 2 * chunk
    key_all = jnp.broadcast_to(key_pos, (length, length))
    return key_all.T >= key_all


def attend_kernel(model_width, orders, *refs):
    parts = refs[: len(orders) + 1]
    (
        query_ref,
        keys_ref,
        values_ref,
        q_gain_ref,
        k_gain_ref,
        cos_ref,
        sin_ref,
        pos_ref,
        attended_ref,
        q_rot_ref,
        k_rot_ref,
        squares_ref,
    ) = refs[len(parts) :]
    for i, row in enumerate(summed_blocks(parts, orders)):
        squares_ref[i : i + 1, :] = row
    rows, width = query_ref.shape
    half = rows // 2
    chunk = SEQ // 2
    for s in range(rows // SEQ):
        every = slice(None)
        cos = sequence_rows(cos_ref, s, chunk, half, every)
        sin = sequence_rows(sin_ref, s, chunk, half, every)
        mask = causal_mask(pos_ref, s, chunk, half)
        count = rows // squares_ref.shape[0]
        blocks = sequence_blocks(squares_ref, s, chunk, count)
        q_inv = inverse_column(squares_ref, 0, blocks, count, model_width)
        k_inv = inverse_column(squares_ref, 1, blocks, count, model_width)
        for h in range(width // HD):
            lanes = slice(h * HD, (h + 1) * HD)
            q = sequence_rows(query_ref, s, chunk, half, lanes) * q_inv * q_gain_ref[:, lanes]
            k = sequence_rows(keys_ref, s, chunk, half, lanes) * k_inv * k_gain_ref[:, lanes]
            q = (q * cos + pltpu.roll(q, HD // 2, 1) * sin).astype(jnp.bfloat16)
            k = (k * cos + pltpu.roll(k, HD // 2, 1) * sin).astype(jnp.bfloat16)
            store_rows(q_rot_ref, s, chunk, half, lanes, q)
            store_rows(k_rot_ref, s, chunk, half, lanes, k)
            scores = times_transposed(q, k) * (1.0 / math.sqrt(HD))
            scores = jnp.where(mask, scores, -1e30)
            shifted = jnp.exp(scores - jnp.max(scores, axis=1, keepdims=True))
            probs = (shifted / jnp.sum(shifted, axis=1, keepdims=True)).astype(jnp.bfloat16)
            v = sequence_rows(values_ref, s, chunk, half, lanes)
            store_rows(
                attended_ref, s, chunk, half, lanes, product(probs, v).astype(jnp.bfloat16)
            )


def attend(query, keys, values, squares, orders, q_gain, k_gain, tables, model_width):
    rows, width = query.shape
    out = jax.ShapeDtypeStruct((rows, width), jnp.bfloat16)
    return pl.pallas_call(
        functools.partial(attend_kernel, model_width, orders),
        out_shape=(
            out,
            out,
            out,
            jax.ShapeDtypeStruct(squares[0].shape, jnp.float32),
        ),
        name="attend",
        compiler_params=pltpu.CompilerParams(vmem_limit_bytes=16 * MIB),
        cost_estimate=pl.CostEstimate(
            flops=4 * rows * SEQ * width,
            bytes_accessed=16 * rows * width,
            transcendentals=rows * SEQ * width // HD,
        ),
    )(*squares, query, keys, values, q_gain[None, :], k_gain[None, :], *tables)


def attend_back_kernel(model_width, pieces, *refs):
    (
        w_out_ref,
        q_rot_ref,
        k_rot_ref,
        values_ref,
        query_ref,
        keys_ref,
        squares_ref,
        q_gain_ref,
        k_gain_ref,
        cos_ref,
        sin_ref,
        pos_ref,
        grad_values_ref,
        grad_q_ref,
        grad_k_ref,
        inner_ref,
        gain_ref,
        grad_ref,
    ) = refs[pieces:]
    rows, width = query_ref.shape
    grad = times_transposed(joined(refs[:pieces]), w_out_ref[...])
    grad_ref[...] = grad.astype(jnp.bfloat16)
    inner_ref[...] = jnp.zeros_like(inner_ref)
    half = rows // 2
    chunk = SEQ // 2
    scale = 1.0 / math.sqrt(HD)
    gain_ref[...] = jnp.zeros_like(gain_ref)
    for s in range(rows // SEQ):
        every = slice(None)
        cos = sequence_rows(cos_ref, s, chunk, half, every)
        sin = sequence_rows(sin_ref, s, chunk, half, every)
        mask = causal_mask(pos_ref, s, chunk, half)
        count = rows // squares_ref.shape[0]
        blocks = sequence_blocks(squares_ref, s, chunk, count)
        q_inv = inverse_column(squares_ref, 0, blocks, count, model_width)
        k_inv = inverse_column(squares_ref, 1, blocks, count, model_width)

        def head(h, inners):
            q_inner, k_inner = inners
            lanes = pl.ds(pl.multiple_of(h * HD, HD), HD)
            q = sequence_rows(q_rot_ref, s, chunk, half, lanes)
            k = sequence_rows(k_rot_ref, s, chunk, half, lanes)
            v = sequence_rows(values_ref, s, chunk, half, lanes)
            g = sequence_rows(grad_ref, s, chunk, half, lanes)
            scores = times_transposed(q, k) * scale
            scores = jnp.where(mask, scores, -1e30)
            shifted = jnp.exp(scores - jnp.max(scores, axis=1, keepdims=True))
            probs = shifted / jnp.sum(shifted, axis=1, keepdims=True)
            grad_v = transposed_times(probs.astype(jnp.bfloat16), g).astype(jnp.bfloat16)
            store_rows(grad_values_ref, s, chunk, half, lanes, grad_v)
            grad_probs = times_transposed(g, v)
            inner = jnp.sum(probs * grad_probs, axis=1, keepdims=True)
            grad_scores = (probs * (grad_probs - inner) * scale).astype(jnp.bfloat16)
            grad_q = product(grad_scores, k)
            grad_k = transposed_times(grad_scores, q)
            grad_q = grad_q * cos - pltpu.roll(grad_q, HD // 2, 1) * sin
            grad_k = grad_k * cos - pltpu.roll(grad_k, HD // 2, 1) * sin
            q_part = grad_q * (sequence_rows(query_ref, s, chunk, half, lanes) * q_inv)
            k_part = grad_k * (sequence_rows(keys_ref, s, chunk, half, lanes) * k_inv)
            gain_ref[0:1, lanes] += jnp.sum(q_part, axis=0, keepdims=True)
            gain_ref[1:2, lanes] += jnp.sum(k_part, axis=0, keepdims=True)
            q_inner = q_inner + row_sums(q_part * q_gain_ref[:, lanes])
            k_inner = k_inner + row_sums(k_part * k_gain_ref[:, lanes])
            store_rows(grad_q_ref, s, chunk, half, lanes, grad_q * q_gain_ref[:, lanes])
            store_rows(grad_k_ref, s, chunk, half, lanes, grad_k * k_gain_ref[:, lanes])
            return q_inner, k_inner

        zero = jnp.zeros((1, SEQ), jnp.float32)
        q_inner, k_inner = lax.fori_loop(0, width // HD, head, (zero, zero))
        store_blocks(inner_ref, 0, blocks, q_inner, count)
        store_blocks(inner_ref, 1, blocks, k_inner, count)


def attend_back(
    grad_attn, w_out, q_rot, k_rot, values, query, keys, squares, q_gain, k_gain, tables, model_width
):
    rows, width = query.shape
    wide = jax.ShapeDtypeStruct((rows, width), jnp.float32)
    return pl.pallas_call(
        functools.partial(attend_back_kernel, model_width, len(grad_attn)),
        out_shape=(
            jax.ShapeDtypeStruct((rows, width), jnp.bfloat16),
            wide,
            wide,
            jax.ShapeDtypeStruct(squares.shape, jnp.float32),
            jax.ShapeDtypeStruct((2, width), jnp.float32),
        ),
        scratch_shapes=[pltpu.VMEM((rows, width), jnp.bfloat16)],
        name="attend_back",
        compiler_params=pltpu.CompilerParams(vmem_limit_bytes=16 * MIB),
        cost_estimate=pl.CostEstimate(
            flops=10 * rows * SEQ * width,
            bytes_accessed=26 * rows * width,
            transcendentals=rows * SEQ * width // HD,
        ),
    )(
        *grad_attn,
        w_out,
        q_rot,
        k_rot,
        values,
        query,
        keys,
        squares,
        q_gain[None, :],
        k_gain[None, :],
        *tables,
    )


def finish_kernel(model_width, orders, *refs):
    parts = refs[: len(orders) + 1]
    (
        query_ref,
        keys_ref,
        grad_q_ref,
        grad_k_ref,
        grad_values_ref,
        squares_ref,
        gains_ref,
        out_ref,
        inner_ref,
        gain_rows_ref,
    ) = refs[len(parts) :]
    rows, width = query_ref.shape
    blocks = list(range(squares_ref.shape[0]))
    count = rows // len(blocks)
    sums = summed_blocks([part.at[: len(blocks)] for part in parts], orders)
    for i, row in enumerate(sums):
        inner_ref[i : i + 1, :] = row
    for i, source, target in ((0, query_ref, grad_q_ref), (1, keys_ref, grad_k_ref)):
        inverse = inverse_column(squares_ref, i, blocks, count, model_width)
        inner = column(block_row(inner_ref, i, blocks, count) / model_width, HD)
        for h in range(width // HD):
            lanes = slice(h * HD, (h + 1) * HD)
            normed = source[:, lanes] * inverse
            value = inverse * (target[:, lanes] - normed * inner)
            start = i * width + h * HD
            out_ref[:rows, start : start + HD] = value.astype(jnp.bfloat16)
    out_ref[:rows, 2 * width :] = grad_values_ref[...]
    rest = [part[len(blocks) :, :] for part in parts]
    while len(rest) > 1:
        rest = [rest[i] + rest[i + 1] for i in range(0, len(rest), 2)]
    rest = rest[0]
    gains = [rest[i : i + 1, :] for i in range(rest.shape[0])]
    for i in range(2):
        gains += [gains_ref[i : i + 1, h * HD : (h + 1) * HD] for h in range(width // HD)]
    gain_rows_ref[...] = jnp.zeros_like(gain_rows_ref)
    across = 3 * width // HD
    half = gain_rows_ref.shape[0] // 2
    for i, gain in enumerate(gains):
        r, lanes = i // across, slice(i % across * HD, (i % across + 1) * HD)
        gain_rows_ref[r : r + 1, lanes] = gain
    high = gain_rows_ref[:half, :].astype(jnp.bfloat16).astype(jnp.float32)
    gain_rows_ref[half:, :] = gain_rows_ref[:half, :] - high
    out_ref[rows:, :] = gain_rows_ref[...].astype(jnp.bfloat16)


def gain_row_count(model_width, width):
    blocks = (2 * model_width + 2 * width) // HD
    return 16 * pl.cdiv(pl.cdiv(blocks, 3 * width // HD), 8)


def finish(query, keys, grad_q, grad_k, grad_values, squares, inner, gains, orders, model_width):
    rows, width = query.shape
    extra = gain_row_count(model_width, width)
    return pl.pallas_call(
        functools.partial(finish_kernel, model_width, orders),
        out_shape=jax.ShapeDtypeStruct((rows + extra, 3 * width), jnp.bfloat16),
        scratch_shapes=[
            pltpu.VMEM(squares.shape, jnp.float32),
            pltpu.VMEM((extra, 3 * width), jnp.float32),
        ],
        name="finish",
        compiler_params=pltpu.CompilerParams(vmem_limit_bytes=16 * MIB),
        cost_estimate=pl.CostEstimate(
            flops=10 * rows * width, bytes_accessed=24 * rows * width, transcendentals=0
        ),
    )(*inner, query, keys, grad_q, grad_k, grad_values, squares, gains)


def sum_gains_kernel(*refs):
    groups = refs[:-4]
    half = groups[0].shape[0] // 2
    values = []
    for ref in groups:
        values.append(ref[:half, :].astype(jnp.float32) + ref[half:, :].astype(jnp.float32))
    while len(values) > 1:
        values = [values[i] + values[i + 1] for i in range(0, len(values), 2)]
    total = values[0]
    across = total.shape[1] // HD
    at = 0
    for out in refs[-4:]:
        for j in range(out.shape[1] // HD):
            r, c = at // across, at % across
            out[:, j * HD : (j + 1) * HD] = total[r : r + 1, c * HD : (c + 1) * HD]
            at += 1


def sum_gains(groups, model_width, width):
    extra = gain_row_count(model_width, width)
    at = [group.shape[0] // extra - 1 for group in groups]
    shapes = [(1, model_width), (1, model_width), (1, width), (1, width)]
    outs = pl.pallas_call(
        sum_gains_kernel,
        grid=(1,),
        in_specs=[pl.BlockSpec((extra, 3 * width), lambda i, j=j: (j, 0)) for j in at],
        out_specs=[pl.BlockSpec(shape, lambda i: (0, 0)) for shape in shapes],
        out_shape=[jax.ShapeDtypeStruct(shape, jnp.float32) for shape in shapes],
        name="sum_gains",
        compiler_params=pltpu.CompilerParams(vmem_limit_bytes=4 * MIB),
    )(*groups)
    return [out[0] for out in outs]


def back_product(grad_ref, weights):
    width = weights[0].shape[1]
    return sum(
        times_transposed(grad_ref[:, i * width : (i + 1) * width], weight[...])
        for i, weight in enumerate(weights)
    )


def far_kernel(grad_ref, *refs):
    refs[-1][...] = back_product(grad_ref, refs[:-1]).astype(jnp.bfloat16)


def near_kernel(count, grad_ref, far_ref, *refs):
    own_ref, others = refs[3], refs[4:]
    total = back_product(grad_ref, refs[:3]) + far_ref[...].astype(jnp.float32)
    own_ref[...] = total[:count]
    for k, ref in enumerate(others):
        ref[...] = total[(k + 1) * count : (k + 2) * count].astype(jnp.bfloat16)


def tokens_back(grad, weights, half, part, far=None, count=None):
    depth, width = weights[0].shape
    tile = min(512, depth)
    specs = [pl.BlockSpec((half, 3 * width), lambda j: (part, 0))]
    arrays = [grad]
    if far is not None:
        specs.append(pl.BlockSpec((half, tile), lambda j: (0, j)))
        arrays.append(far)
    specs += [pl.BlockSpec((tile, width), lambda j: (j, 0))] * 3
    if far is None:
        kernel, sizes = far_kernel, [(half, jnp.bfloat16)]
    else:
        kernel = functools.partial(near_kernel, count)
        sizes = [(count, jnp.float32)] + [(count, jnp.bfloat16)] * (half // count - 1)
    return pl.pallas_call(
        kernel,
        grid=(depth // tile,),
        in_specs=specs,
        out_specs=[pl.BlockSpec((size, tile), lambda j: (0, j)) for size, _ in sizes],
        out_shape=[jax.ShapeDtypeStruct((size, depth), kind) for size, kind in sizes],
        name="tokens_back",
        compiler_params=pltpu.CompilerParams(vmem_limit_bytes=16 * MIB),
        cost_estimate=pl.CostEstimate(
            flops=6 * half * depth * width,
            bytes_accessed=6 * depth * width + 8 * half * depth,
            transcendentals=0,
        ),
    )(*arrays, *weights)


def out_grad_kernel(pieces, *refs):
    attended_ref, me_ref = refs[pieces : pieces + 2]
    own_ref, others, grad_ref = refs[pieces + 2], refs[pieces + 3 : -1], refs[-1]
    count = own_ref.shape[0]
    grad_ref[...] = transposed_times(attended_ref[...], joined(refs[:pieces]))
    me = me_ref[0]
    own_ref[...] = grad_ref[pl.ds(pl.multiple_of(me * count, count), count), :]
    for j, ref in enumerate(others):
        start = pl.multiple_of((me ^ (j + 1)) * count, count)
        ref[...] = grad_ref[pl.ds(start, count), :].astype(jnp.bfloat16)


def out_grad(attended, grad_attn, me, dp_size):
    width, depth = attended.shape[1], grad_attn[0].shape[1]
    piece = (width // dp_size, depth)
    return pl.pallas_call(
        functools.partial(out_grad_kernel, len(grad_attn)),
        in_specs=[pl.BlockSpec(array.shape, lambda: (0, 0)) for array in (*grad_attn, attended)]
        + [pl.BlockSpec(memory_space=pltpu.SMEM)],
        out_shape=[jax.ShapeDtypeStruct(piece, jnp.float32)]
        + [jax.ShapeDtypeStruct(piece, jnp.bfloat16)] * (dp_size - 1),
        scratch_shapes=[pltpu.VMEM((width, depth), jnp.float32)],
        name="out_grad",
        compiler_params=pltpu.CompilerParams(vmem_limit_bytes=16 * MIB),
        cost_estimate=pl.CostEstimate(
            flops=2 * attended.shape[0] * width * depth,
            bytes_accessed=2 * attended.shape[0] * (width + depth) + 3 * width * depth,
            transcendentals=0,
        ),
    )(*grad_attn, attended, me)


def assemble_kernel(*refs):
    me = refs[-2][0]
    out_ref = refs[-1]
    for j, ref in enumerate(refs[:-2]):
        count = ref.shape[0]
        start = pl.multiple_of((me ^ j) * count, count)
        out_ref[pl.ds(start, count), :] = ref[...].astype(jnp.float32)


def assemble(pieces, me):
    count, depth = pieces[0].shape
    return pl.pallas_call(
        assemble_kernel,
        in_specs=[pl.BlockSpec((count, depth), lambda: (0, 0)) for _ in pieces]
        + [pl.BlockSpec(memory_space=pltpu.SMEM)],
        out_shape=jax.ShapeDtypeStruct((len(pieces) * count, depth), jnp.float32),
        name="assemble",
        compiler_params=pltpu.CompilerParams(vmem_limit_bytes=8 * MIB),
    )(*pieces, me)


def summed_blocks(refs, orders):
    rows = []
    for i in range(refs[0].shape[0]):
        total = refs[0][i : i + 1, :]
        for order, other in zip(orders, refs[1:]):
            total = total + other[order[i] : order[i] + 1, :]
        rows.append(total)
    return rows


def add_blocks_kernel(orders, *refs):
    own, others, out = refs[0], refs[1:-1], refs[-1]
    count = len(orders[0])
    for i in range(count):
        total = own[i : i + 1, :]
        for order, other in zip(orders, others):
            total = total + other[order[i] : order[i] + 1, :]
        out[i : i + 1, :] = total
    if own.shape[0] > count:
        rest = [own[count:, :]] + [other[count:, :] for other in others]
        while len(rest) > 1:
            rest = [rest[i] + rest[i + 1] for i in range(0, len(rest), 2)]
        out[count:, :] = rest[0]


def add_pieces_kernel(*refs):
    total = refs[0][...]
    for ref in refs[1:-1]:
        total = total + ref[...].astype(jnp.float32)
    refs[-1][...] = total.astype(jnp.bfloat16)


def add_pieces(own, others):
    return pl.pallas_call(
        add_pieces_kernel,
        out_shape=jax.ShapeDtypeStruct(own.shape, jnp.bfloat16),
        name="add_pieces",
        compiler_params=pltpu.CompilerParams(vmem_limit_bytes=4 * MIB),
    )(own, *others)


def add_blocks(own, others, orders):
    return pl.pallas_call(
        functools.partial(add_blocks_kernel, orders),
        out_shape=jax.ShapeDtypeStruct(own.shape, own.dtype),
        name="add_blocks",
        compiler_params=pltpu.CompilerParams(vmem_limit_bytes=4 * MIB),
    )(own, *others)


def in_hbm(array):
    return pltpu.with_memory_space_constraint(array, pltpu.HBM)


def resident(shape):
    return pl.BlockSpec(shape, lambda i: (0, 0), pipeline_mode=pl.Buffered(1))


def joined(refs):
    return refs[0][...] if len(refs) == 1 else jnp.concatenate([r[...] for r in refs], axis=0)


def project_kernel(pieces, *refs):
    rows = joined(refs[:pieces])
    w_query_ref, w_key_ref, w_value_ref, query_ref, keys_ref, values_ref, squares_ref = refs[
        pieces:
    ]
    blocks = list(range(squares_ref.shape[0]))
    count = rows.shape[0] // len(blocks)
    if 2 * count < squares_ref.shape[1]:
        squares_ref[...] = jnp.zeros_like(squares_ref)
    for i, weight, out in ((0, w_query_ref, query_ref), (1, w_key_ref, keys_ref)):
        value = product(rows, weight[...])
        out[...] = value
        square = value * value
        folded = square[:, :HD]
        for h in range(1, value.shape[1] // HD):
            folded = folded + square[:, h * HD : (h + 1) * HD]
        store_blocks(squares_ref, i, blocks, row_sums(folded), count)
    values_ref[...] = product(rows, w_value_ref[...]).astype(jnp.bfloat16)


def project(rows, w_query, w_key, w_value, tensor_size):
    count = sum(piece.shape[0] for piece in rows)
    depth, width = w_query.shape
    wide = jax.ShapeDtypeStruct((count, width), jnp.float32)
    return pl.pallas_call(
        functools.partial(project_kernel, len(rows)),
        out_shape=(
            wide,
            wide,
            jax.ShapeDtypeStruct((count, width), jnp.bfloat16),
            jax.ShapeDtypeStruct((tensor_size, max(HD, 2 * count // tensor_size)), jnp.float32),
        ),
        name="project",
        compiler_params=pltpu.CompilerParams(vmem_limit_bytes=16 * MIB),
        cost_estimate=pl.CostEstimate(
            flops=6 * count * depth * width,
            bytes_accessed=2 * count * depth + 6 * depth * width + 10 * count * width,
            transcendentals=0,
        ),
    )(*[in_hbm(array) for array in (*rows, w_query, w_key, w_value)])


def ffn_kernel(pieces, *refs):
    rows = joined(refs[:pieces])
    w_gate_ref, w_up_ref, gate_ref, up_ref, swiglu_ref = refs[pieces:]
    gate = product(rows, w_gate_ref[...])
    up = product(rows, w_up_ref[...])
    gate_ref[...] = gate.astype(jnp.bfloat16)
    up_ref[...] = up.astype(jnp.bfloat16)
    swiglu_ref[...] = (gate * jax.nn.sigmoid(gate) * up).astype(jnp.bfloat16)


def ffn(rows, w_gate, w_up):
    count = sum(piece.shape[0] for piece in rows)
    depth, units = w_gate.shape
    tile = min(256, units)
    weight = pl.BlockSpec((depth, tile), lambda j: (0, j))
    out = pl.BlockSpec((count, tile), lambda j: (0, j))
    wide = jax.ShapeDtypeStruct((count, units), jnp.bfloat16)
    return pl.pallas_call(
        functools.partial(ffn_kernel, len(rows)),
        grid=(units // tile,),
        in_specs=[resident(piece.shape) for piece in rows]
        + [weight, weight],
        out_specs=(out, out, out),
        out_shape=(wide, wide, jax.ShapeDtypeStruct((count, units), jnp.bfloat16)),
        name="ffn",
        compiler_params=pltpu.CompilerParams(vmem_limit_bytes=16 * MIB),
        cost_estimate=pl.CostEstimate(
            flops=4 * count * depth * units,
            bytes_accessed=2 * count * depth + 4 * depth * units + 10 * count * units,
            transcendentals=count * units,
        ),
    )(*rows, w_gate, w_up)


def ffn_back_kernel(pieces, *refs):
    grad = joined(refs[:pieces])
    w_down_ref, gate_ref, up_ref, grad_gate_ref, grad_up_ref = refs[pieces:]
    grad_swiglu = times_transposed(grad, w_down_ref[...])
    gate = gate_ref[...].astype(jnp.float32)
    sig = jax.nn.sigmoid(gate)
    grad_gate = grad_swiglu * up_ref[...].astype(jnp.float32) * sig * (1.0 + gate * (1.0 - sig))
    grad_gate_ref[...] = grad_gate.astype(jnp.bfloat16)
    grad_up_ref[...] = (grad_swiglu * (gate * sig)).astype(jnp.bfloat16)


def ffn_back(grad, w_down, gate, up, place=lambda array: array):
    count = sum(piece.shape[0] for piece in grad)
    units, depth = w_down.shape
    tile = min(256, units)
    out = pl.BlockSpec((count, tile), lambda j: (0, j))
    narrow = jax.ShapeDtypeStruct((count, units), jnp.bfloat16)
    return pl.pallas_call(
        functools.partial(ffn_back_kernel, len(grad)),
        grid=(units // tile,),
        in_specs=[resident(piece.shape) for piece in grad]
        + [pl.BlockSpec((tile, depth), lambda j: (j, 0)), out, out],
        out_specs=(out, out),
        out_shape=(narrow, narrow),
        name="ffn_back",
        compiler_params=pltpu.CompilerParams(vmem_limit_bytes=16 * MIB),
        cost_estimate=pl.CostEstimate(
            flops=2 * count * depth * units,
            bytes_accessed=2 * count * depth + 2 * depth * units + 12 * count * units,
            transcendentals=count * units,
        ),
    )(*grad, *[place(array) for array in (w_down, gate, up)])


def weight_grad_kernel(left_counts, right_counts, rights, outs, *refs):
    groups = len(left_counts)
    left, at = [], 0
    for count in left_counts:
        left.append(joined(refs[at : at + count]))
        at += count
    out_refs = refs[len(refs) - rights * outs :]
    for r in range(rights):
        right = []
        for count in right_counts:
            right.append(refs[at : at + count])
            at += count
        width = right[0][0].shape[1] // outs
        for o in range(outs):
            sums = []
            for g in range(groups):
                pieces = [ref[:, o * width : (o + 1) * width] for ref in right[g]]
                whole = pieces[0] if len(pieces) == 1 else jnp.concatenate(pieces, axis=0)
                sums.append(transposed_times(left[g], whole))
            while len(sums) > 1:
                sums = [sums[i] - sums[i + 1] * -1.0 for i in range(0, len(sums), 2)]
            out_refs[r * outs + o][...] = sums[0]


def weight_grad(left, *rights, outs=1, extra=0):
    depth = left[0][0].shape[1]
    left_pieces = [piece for group in left for piece in group]
    right_pieces, counts = [], []
    for right in rights:
        for group in right:
            right_pieces += group
            counts += [piece.shape[0] for piece in group[:-1]] + [group[-1].shape[0] - extra]
    rows = sum(piece.shape[0] for piece in left_pieces)
    widths = [right[0][0].shape[1] // outs for right in rights for _ in range(outs)]
    tile = min(512 if max(widths) <= 1024 else 256, depth)
    blocks = 4 * rows * tile + (2 * len(rights)) * rows * rights[0][0][0].shape[1]
    needed = blocks + 4 * tile * sum(widths) * (2 + len(left)) + 4 * MIB
    return pl.pallas_call(
        functools.partial(
            weight_grad_kernel,
            [len(group) for group in left],
            [len(group) for group in rights[0]],
            len(rights),
            outs,
        ),
        grid=(depth // tile,),
        in_specs=[pl.BlockSpec((piece.shape[0], tile), lambda i: (0, i)) for piece in left_pieces]
        + [
            resident((count, piece.shape[1])) for count, piece in zip(counts, right_pieces)
        ],
        out_specs=[pl.BlockSpec((tile, width), lambda i: (i, 0)) for width in widths],
        out_shape=[jax.ShapeDtypeStruct((depth, width), jnp.float32) for width in widths],
        name="weight_grad",
        compiler_params=pltpu.CompilerParams(vmem_limit_bytes=max(28 * MIB, needed)),
        cost_estimate=pl.CostEstimate(
            flops=2 * rows * depth * sum(widths),
            bytes_accessed=2 * rows * (depth + sum(widths)) + 4 * depth * sum(widths),
            transcendentals=0,
        ),
    )(*[in_hbm(piece) for piece in left_pieces], *right_pieces)


def build(dp_size, tensor_size):
    pairs = tensor_size // 2

    def swap(value, axis, mask):
        size = dp_size if axis == "dp" else tensor_size
        return lax.ppermute(value, axis, [(i, i ^ mask) for i in range(size)])

    def tensor_gather(own, relay=False):
        near = [own]
        for k in range(1, pairs):
            if relay and k == 3:
                near.append(swap(near[2], "tensor", 2))
            else:
                near.append(swap(own, "tensor", 2 * k))
        return near + [swap(near[k], "tensor", 1) for k in range(pairs)]

    def tensor_scatter(partial_of, rows, relay=False):
        half = rows // 2
        far = partial_of(half, rows).astype(jnp.bfloat16)
        far = swap(far, "tensor", 1)
        near = partial_of(0, half) + far.astype(jnp.float32)
        count = half // pairs
        total = near[:count]
        if relay and pairs == 4:
            one, two, three = [near[k * count : (k + 1) * count] for k in range(1, pairs)]
            three = swap(three.astype(jnp.bfloat16), "tensor", 2)
            one = swap(one.astype(jnp.bfloat16), "tensor", 2)
            two = (two + three.astype(jnp.float32)).astype(jnp.bfloat16)
            two = swap(two, "tensor", 4)
            return total + one.astype(jnp.float32) + two.astype(jnp.float32)
        for k in range(1, pairs):
            block = near[k * count : (k + 1) * count].astype(jnp.bfloat16)
            total = total + swap(block, "tensor", 2 * k).astype(jnp.float32)
        return total

    def row_sum(value):
        def order(mask):
            out = []
            for i in range(tensor_size):
                wanted = (2 * (i % pairs) + i // pairs) ^ mask
                out.append((wanted % 2) * pairs + wanted // 2)
            return out

        value = add_blocks(value, [swap(value, "tensor", 1)], [order(1)])
        others = [swap(value, "tensor", 2 * k) for k in range(1, pairs)]
        return [value] + others, [order(2 * k) for k in range(1, pairs)]

    def dp_gather(own, cut):
        if dp_size == 4:
            one = swap(own, "dp", 1)
            two = swap(own, "dp", 2)
            top = one[:cut]
            bottom = two[cut:]
            top = swap(top, "dp", 2)
            bottom = swap(bottom, "dp", 1)
            return [[own], [one], [two], [top, bottom]]
        return [[own]] + [[swap(own, "dp", j)] for j in range(1, dp_size)]

    def dp_gather_shared(pieces):
        near = jnp.concatenate(pieces[:pairs], axis=0)
        fetched = dp_gather(near, near.shape[0] // 2)[1:]
        groups = [[near] + pieces[pairs:]]
        for mine in fetched:
            groups.append(mine + [swap(piece, "tensor", 1) for piece in mine])
        return groups

    def dp_sum(own, others, me):
        others = [swap(piece, "dp", j + 1) for j, piece in enumerate(others)]
        total = add_pieces(own, others)
        pieces = [total] + [swap(total, "dp", j) for j in range(1, dp_size)]
        return assemble(pieces, me)

    def positions(rows):
        count = rows // tensor_size
        index = jnp.arange(rows, dtype=jnp.int32)
        block = index // count
        mask = 2 * (block % pairs) + block // pairs
        owner = lax.axis_index("tensor").astype(jnp.int32) ^ mask
        return (owner * count + index % count) % SEQ

    def tables_of(rows):
        pos = positions(rows)
        half_width = HD // 2
        exponent = jnp.arange(half_width, dtype=jnp.float32) * (2.0 / HD)
        frequency = rope_base ** (-exponent)
        angles = pos.astype(jnp.float32)[:, None] * frequency[None, :]
        cos, sin = jnp.cos(angles), jnp.sin(angles)
        return (
            jnp.concatenate([cos, cos], axis=1),
            jnp.concatenate([-sin, sin], axis=1),
            pos[None, :],
        )

    def shards(
        tokens,
        cotangent,
        w_query,
        w_key,
        w_value,
        w_out,
        w_gate,
        w_up,
        w_down,
        q_gain,
        k_gain,
        attn_gain,
        ffn_gain,
    ):
        model_width = tokens.shape[1]
        rows = tokens.shape[0] * tensor_size
        width = w_query.shape[1]
        tables = tables_of(rows)

        gathered = tensor_gather(tokens, relay=True)
        query, keys, values, squares = project(gathered, w_query, w_key, w_value, tensor_size)
        square_parts, orders = row_sum(squares)
        attended, q_rot, k_rot, squares = attend(
            query, keys, values, square_parts, orders, q_gain, k_gain, tables, model_width
        )
        attn_rows = tensor_scatter(lambda a, b: product(attended[a:b], w_out), rows, relay=True)
        a_inverse = row_scale(attn_rows)
        a_normed = attn_rows * a_inverse
        mixed = tokens.astype(jnp.float32) + a_normed * attn_gain
        mixed_b = tensor_gather(mixed.astype(jnp.bfloat16), relay=True)
        gate, up_proj, swiglu = ffn(mixed_b, w_gate, w_up)
        ffn_rows = tensor_scatter(lambda a, b: product(swiglu[a:b], w_down), rows, relay=True)
        m_inverse = row_scale(ffn_rows)
        m_normed = ffn_rows * m_inverse
        layer_out = mixed + m_normed * ffn_gain
        grad_out = cotangent.astype(jnp.float32)
        ffn_gain_part = jnp.sum(grad_out * m_normed, axis=0)
        grad_ffn = tensor_gather(
            norm_back(grad_out * ffn_gain, m_normed, m_inverse).astype(jnp.bfloat16), relay=True
        )
        grad_gate, grad_up = ffn_back(grad_ffn, w_down, gate, up_proj)
        grad_mixed = grad_out + tensor_scatter(
            lambda a, b: times_transposed(grad_gate[a:b], w_gate)
            + times_transposed(grad_up[a:b], w_up),
            rows,
            relay=True,
        )
        attn_gain_part = jnp.sum(grad_mixed * a_normed, axis=0)
        grad_attn = tensor_gather(
            norm_back(grad_mixed * attn_gain, a_normed, a_inverse).astype(jnp.bfloat16), relay=True
        )
        me = lax.axis_index("dp").astype(jnp.int32).reshape(1)
        grad_values, grad_q, grad_k, inner, gain_parts = attend_back(
            grad_attn,
            w_out,
            q_rot,
            k_rot,
            values,
            query,
            keys,
            squares,
            q_gain,
            k_gain,
            tables,
            model_width,
        )
        lanes = inner.shape[1]
        inner_parts, orders = row_sum(
            jnp.concatenate(
                [inner, attn_gain_part.reshape(-1, lanes), ffn_gain_part.reshape(-1, lanes)]
            ),
        )
        out_own, *out_others = out_grad(attended, grad_attn, me, dp_size)
        grad_qkv = finish(
            query,
            keys,
            grad_q,
            grad_k,
            grad_values,
            squares,
            inner_parts,
            gain_parts,
            orders,
            model_width,
        )
        weights = (w_query, w_key, w_value)
        (far,) = tokens_back(grad_qkv, weights, rows // 2, 1)
        far = swap(far, "tensor", 1)
        own, *others = tokens_back(
            grad_qkv, weights, rows // 2, 0, far, tokens.shape[0]
        )
        others = [swap(piece, "tensor", 2 * k + 2) for k, piece in enumerate(others)]
        grad_tokens = grad_mixed + sum([piece.astype(jnp.float32) for piece in others], own)

        tokens_all = dp_gather_shared(gathered)
        mixed_all = dp_gather_shared(mixed_b)
        grad_ffn_all = dp_gather_shared(grad_ffn)
        swiglus, grad_gates, grad_ups = [[swiglu]], [[grad_gate]], [[grad_up]]
        for j in range(1, dp_size):
            gate_j, up_j, swiglu_j = ffn(mixed_all[j], w_gate, w_up)
            grad_gate_j, grad_up_j = ffn_back(
                grad_ffn_all[j], w_down, gate_j, up_j, *[in_hbm][: j // (dp_size - 1)]
            )
            swiglus.append([swiglu_j])
            grad_gates.append([grad_gate_j])
            grad_ups.append([grad_up_j])
        (grad_w_down,) = weight_grad(swiglus, grad_ffn_all)
        (grad_w_gate,) = weight_grad(mixed_all, grad_gates)
        (grad_w_up,) = weight_grad(mixed_all, grad_ups)
        grad_w_out = dp_sum(out_own, out_others, me)
        operands = dp_gather(grad_qkv, rows // 2)
        grad_w_query, grad_w_key, grad_w_value = weight_grad(
            tokens_all, operands, outs=3, extra=grad_qkv.shape[0] - rows
        )
        gains = sum_gains([group[-1] for group in operands], model_width, width)
        return (
            layer_out,
            grad_tokens,
            grad_w_query,
            grad_w_key,
            grad_w_value,
            grad_w_out,
            grad_w_gate,
            grad_w_up,
            grad_w_down,
            gains[2],
            gains[3],
            gains[0],
            gains[1],
        )

    return shards


def solution(mesh):
    placed = (
        P(("dp", "tensor"), None),
        P(("dp", "tensor"), None),
        P(None, "tensor"),
        P(None, "tensor"),
        P(None, "tensor"),
        P("tensor", None),
        P(None, "tensor"),
        P(None, "tensor"),
        P("tensor", None),
        P("tensor"),
        P("tensor"),
        P(),
        P(),
    )
    return jax.shard_map(
        build(mesh.shape["dp"], mesh.shape["tensor"]),
        mesh=mesh,
        in_specs=placed,
        out_specs=(
            P(("dp", "tensor"), None),
            P(("dp", "tensor"), None),
            P(None, "tensor"),
            P(None, "tensor"),
            P(None, "tensor"),
            P("tensor", None),
            P(None, "tensor"),
            P(None, "tensor"),
            P("tensor", None),
            P("tensor"),
            P("tensor"),
            P(),
            P(),
        ),
        check_vma=False,
    )
```

```python
import functools
import math

import jax
import jax.numpy as jnp
from jax import lax
from jax.experimental import pallas as pl
from jax.experimental.pallas import tpu as pltpu
from jax.sharding import PartitionSpec as P

HD = 128
SEQ = 256

epsilon = 1e-06
rope_base = 500000.0

MIB = 1 << 20


def row_scale(matrix):
    return lax.rsqrt(jnp.mean(matrix * matrix, axis=1, keepdims=True) + epsilon)


def norm_back(grad_normed, normed, inverse):
    return inverse * (grad_normed - normed * jnp.mean(grad_normed * normed, axis=1, keepdims=True))


def product(left, right):
    return jnp.dot(left, right, preferred_element_type=jnp.float32)


def times_transposed(left, right):
    return lax.dot_general(
        left, right, (((1,), (1,)), ((), ())), preferred_element_type=jnp.float32
    )


def transposed_times(left, right):
    return lax.dot_general(
        left, right, (((0,), (0,)), ((), ())), preferred_element_type=jnp.float32
    )


def column(row, width):
    return jnp.broadcast_to(row, (width, row.shape[1])).T


def row_sums(matrix):
    return jnp.sum(matrix.T, axis=0, keepdims=True)


def sequence_rows(ref, s, chunk, half, lanes):
    top = ref[s * chunk : (s + 1) * chunk, lanes]
    bottom = ref[half + s * chunk : half + (s + 1) * chunk, lanes]
    return jnp.concatenate([top, bottom], axis=0)


def store_rows(ref, s, chunk, half, lanes, value):
    ref[s * chunk : (s + 1) * chunk, lanes] = value[:chunk]
    ref[half + s * chunk : half + (s + 1) * chunk, lanes] = value[chunk:]


def block_row(ref, i, blocks, count):
    return jnp.concatenate(
        [ref[b : b + 1, i * count : (i + 1) * count] for b in blocks], axis=1
    )


def sequence_blocks(ref, s, chunk, count):
    steps = chunk // count
    pairs = ref.shape[0] // 2
    return [h * pairs + s * steps + k for h in range(2) for k in range(steps)]


def store_blocks(ref, i, blocks, row, count):
    for j, b in enumerate(blocks):
        ref[b : b + 1, i * count : (i + 1) * count] = row[:, j * count : (j + 1) * count]


def inverse_column(squares_ref, i, blocks, count, model_width):
    squares = block_row(squares_ref, i, blocks, count)
    return column(lax.rsqrt(squares / model_width + epsilon), HD)


def causal_mask(pos_ref, s, chunk, half):
    key_pos = jnp.concatenate(
        [
            pos_ref[:, s * chunk : (s + 1) * chunk],
            pos_ref[:, half + s * chunk : half + (s + 1) * chunk],
        ],
        axis=1,
    )
    length = 2 * chunk
    key_all = jnp.broadcast_to(key_pos, (length, length))
    return key_all.T >= key_all


def attend_kernel(model_width, orders, *refs):
    parts = refs[: len(orders) + 1]
    (
        query_ref,
        keys_ref,
        values_ref,
        q_gain_ref,
        k_gain_ref,
        cos_ref,
        sin_ref,
        pos_ref,
        attended_ref,
        q_rot_ref,
        k_rot_ref,
        squares_ref,
    ) = refs[len(parts) :]
    for i, row in enumerate(summed_blocks(parts, orders)):
        squares_ref[i : i + 1, :] = row
    rows, width = query_ref.shape
    half = rows // 2
    chunk = SEQ // 2
    for s in range(rows // SEQ):
        every = slice(None)
        cos = sequence_rows(cos_ref, s, chunk, half, every)
        sin = sequence_rows(sin_ref, s, chunk, half, every)
        mask = causal_mask(pos_ref, s, chunk, half)
        count = rows // squares_ref.shape[0]
        blocks = sequence_blocks(squares_ref, s, chunk, count)
        q_inv = inverse_column(squares_ref, 0, blocks, count, model_width)
        k_inv = inverse_column(squares_ref, 1, blocks, count, model_width)
        for h in range(width // HD):
            lanes = slice(h * HD, (h + 1) * HD)
            q = sequence_rows(query_ref, s, chunk, half, lanes) * q_inv * q_gain_ref[:, lanes]
            k = sequence_rows(keys_ref, s, chunk, half, lanes) * k_inv * k_gain_ref[:, lanes]
            q = (q * cos + pltpu.roll(q, HD // 2, 1) * sin).astype(jnp.bfloat16)
            k = (k * cos + pltpu.roll(k, HD // 2, 1) * sin).astype(jnp.bfloat16)
            store_rows(q_rot_ref, s, chunk, half, lanes, q)
            store_rows(k_rot_ref, s, chunk, half, lanes, k)
            scores = times_transposed(q, k) * (1.0 / math.sqrt(HD))
            scores = jnp.where(mask, scores, -1e30)
            shifted = jnp.exp(scores - jnp.max(scores, axis=1, keepdims=True))
            probs = (shifted / jnp.sum(shifted, axis=1, keepdims=True)).astype(jnp.bfloat16)
            v = sequence_rows(values_ref, s, chunk, half, lanes)
            store_rows(
                attended_ref, s, chunk, half, lanes, product(probs, v).astype(jnp.bfloat16)
            )


def attend(query, keys, values, squares, orders, q_gain, k_gain, tables, model_width):
    rows, width = query.shape
    out = jax.ShapeDtypeStruct((rows, width), jnp.bfloat16)
    return pl.pallas_call(
        functools.partial(attend_kernel, model_width, orders),
        out_shape=(
            out,
            out,
            out,
            jax.ShapeDtypeStruct(squares[0].shape, jnp.float32),
        ),
        name="attend",
        compiler_params=pltpu.CompilerParams(vmem_limit_bytes=16 * MIB),
        cost_estimate=pl.CostEstimate(
            flops=4 * rows * SEQ * width,
            bytes_accessed=16 * rows * width,
            transcendentals=rows * SEQ * width // HD,
        ),
    )(*squares, query, keys, values, q_gain[None, :], k_gain[None, :], *tables)


def attend_back_kernel(model_width, pieces, *refs):
    (
        w_out_ref,
        q_rot_ref,
        k_rot_ref,
        values_ref,
        query_ref,
        keys_ref,
        squares_ref,
        q_gain_ref,
        k_gain_ref,
        cos_ref,
        sin_ref,
        pos_ref,
        grad_values_ref,
        grad_q_ref,
        grad_k_ref,
        inner_ref,
        gain_ref,
        grad_ref,
    ) = refs[pieces:]
    rows, width = query_ref.shape
    grad = times_transposed(joined(refs[:pieces]), w_out_ref[...])
    grad_ref[...] = grad.astype(jnp.bfloat16)
    inner_ref[...] = jnp.zeros_like(inner_ref)
    half = rows // 2
    chunk = SEQ // 2
    scale = 1.0 / math.sqrt(HD)
    gain_ref[...] = jnp.zeros_like(gain_ref)
    for s in range(rows // SEQ):
        every = slice(None)
        cos = sequence_rows(cos_ref, s, chunk, half, every)
        sin = sequence_rows(sin_ref, s, chunk, half, every)
        mask = causal_mask(pos_ref, s, chunk, half)
        count = rows // squares_ref.shape[0]
        blocks = sequence_blocks(squares_ref, s, chunk, count)
        q_inv = inverse_column(squares_ref, 0, blocks, count, model_width)
        k_inv = inverse_column(squares_ref, 1, blocks, count, model_width)

        def head(h, inners):
            q_inner, k_inner = inners
            lanes = pl.ds(pl.multiple_of(h * HD, HD), HD)
            q = sequence_rows(q_rot_ref, s, chunk, half, lanes)
            k = sequence_rows(k_rot_ref, s, chunk, half, lanes)
            v = sequence_rows(values_ref, s, chunk, half, lanes)
            g = sequence_rows(grad_ref, s, chunk, half, lanes)
            scores = times_transposed(q, k) * scale
            scores = jnp.where(mask, scores, -1e30)
            shifted = jnp.exp(scores - jnp.max(scores, axis=1, keepdims=True))
            probs = shifted / jnp.sum(shifted, axis=1, keepdims=True)
            grad_v = transposed_times(probs.astype(jnp.bfloat16), g).astype(jnp.bfloat16)
            store_rows(grad_values_ref, s, chunk, half, lanes, grad_v)
            grad_probs = times_transposed(g, v)
            inner = jnp.sum(probs * grad_probs, axis=1, keepdims=True)
            grad_scores = (probs * (grad_probs - inner) * scale).astype(jnp.bfloat16)
            grad_q = product(grad_scores, k)
            grad_k = transposed_times(grad_scores, q)
            grad_q = grad_q * cos - pltpu.roll(grad_q, HD // 2, 1) * sin
            grad_k = grad_k * cos - pltpu.roll(grad_k, HD // 2, 1) * sin
            q_part = grad_q * (sequence_rows(query_ref, s, chunk, half, lanes) * q_inv)
            k_part = grad_k * (sequence_rows(keys_ref, s, chunk, half, lanes) * k_inv)
            gain_ref[0:1, lanes] += jnp.sum(q_part, axis=0, keepdims=True)
            gain_ref[1:2, lanes] += jnp.sum(k_part, axis=0, keepdims=True)
            q_inner = q_inner + row_sums(q_part * q_gain_ref[:, lanes])
            k_inner = k_inner + row_sums(k_part * k_gain_ref[:, lanes])
            store_rows(grad_q_ref, s, chunk, half, lanes, grad_q * q_gain_ref[:, lanes])
            store_rows(grad_k_ref, s, chunk, half, lanes, grad_k * k_gain_ref[:, lanes])
            return q_inner, k_inner

        zero = jnp.zeros((1, SEQ), jnp.float32)
        q_inner, k_inner = lax.fori_loop(0, width // HD, head, (zero, zero))
        store_blocks(inner_ref, 0, blocks, q_inner, count)
        store_blocks(inner_ref, 1, blocks, k_inner, count)


def attend_back(
    grad_attn, w_out, q_rot, k_rot, values, query, keys, squares, q_gain, k_gain, tables, model_width
):
    rows, width = query.shape
    wide = jax.ShapeDtypeStruct((rows, width), jnp.float32)
    return pl.pallas_call(
        functools.partial(attend_back_kernel, model_width, len(grad_attn)),
        out_shape=(
            jax.ShapeDtypeStruct((rows, width), jnp.bfloat16),
            wide,
            wide,
            jax.ShapeDtypeStruct(squares.shape, jnp.float32),
            jax.ShapeDtypeStruct((2, width), jnp.float32),
        ),
        scratch_shapes=[pltpu.VMEM((rows, width), jnp.bfloat16)],
        name="attend_back",
        compiler_params=pltpu.CompilerParams(vmem_limit_bytes=16 * MIB),
        cost_estimate=pl.CostEstimate(
            flops=10 * rows * SEQ * width,
            bytes_accessed=26 * rows * width,
            transcendentals=rows * SEQ * width // HD,
        ),
    )(
        *grad_attn,
        w_out,
        q_rot,
        k_rot,
        values,
        query,
        keys,
        squares,
        q_gain[None, :],
        k_gain[None, :],
        *tables,
    )


def finish_kernel(model_width, orders, *refs):
    parts = refs[: len(orders) + 1]
    (
        query_ref,
        keys_ref,
        grad_q_ref,
        grad_k_ref,
        grad_values_ref,
        squares_ref,
        gains_ref,
        out_ref,
        inner_ref,
        gain_rows_ref,
    ) = refs[len(parts) :]
    rows, width = query_ref.shape
    blocks = list(range(squares_ref.shape[0]))
    count = rows // len(blocks)
    sums = summed_blocks([part.at[: len(blocks)] for part in parts], orders)
    for i, row in enumerate(sums):
        inner_ref[i : i + 1, :] = row
    for i, source, target in ((0, query_ref, grad_q_ref), (1, keys_ref, grad_k_ref)):
        inverse = inverse_column(squares_ref, i, blocks, count, model_width)
        inner = column(block_row(inner_ref, i, blocks, count) / model_width, HD)
        for h in range(width // HD):
            lanes = slice(h * HD, (h + 1) * HD)
            normed = source[:, lanes] * inverse
            value = inverse * (target[:, lanes] - normed * inner)
            start = i * width + h * HD
            out_ref[:rows, start : start + HD] = value.astype(jnp.bfloat16)
    out_ref[:rows, 2 * width :] = grad_values_ref[...]
    rest = [part[len(blocks) :, :] for part in parts]
    while len(rest) > 1:
        rest = [rest[i] + rest[i + 1] for i in range(0, len(rest), 2)]
    rest = rest[0]
    gains = [rest[i : i + 1, :] for i in range(rest.shape[0])]
    for i in range(2):
        gains += [gains_ref[i : i + 1, h * HD : (h + 1) * HD] for h in range(width // HD)]
    gain_rows_ref[...] = jnp.zeros_like(gain_rows_ref)
    across = 3 * width // HD
    half = gain_rows_ref.shape[0] // 2
    for i, gain in enumerate(gains):
        r, lanes = i // across, slice(i % across * HD, (i % across + 1) * HD)
        gain_rows_ref[r : r + 1, lanes] = gain
    high = gain_rows_ref[:half, :].astype(jnp.bfloat16).astype(jnp.float32)
    gain_rows_ref[half:, :] = gain_rows_ref[:half, :] - high
    out_ref[rows:, :] = gain_rows_ref[...].astype(jnp.bfloat16)


def gain_row_count(model_width, width):
    blocks = (2 * model_width + 2 * width) // HD
    return 16 * pl.cdiv(pl.cdiv(blocks, 3 * width // HD), 8)


def finish(query, keys, grad_q, grad_k, grad_values, squares, inner, gains, orders, model_width):
    rows, width = query.shape
    extra = gain_row_count(model_width, width)
    return pl.pallas_call(
        functools.partial(finish_kernel, model_width, orders),
        out_shape=jax.ShapeDtypeStruct((rows + extra, 3 * width), jnp.bfloat16),
        scratch_shapes=[
            pltpu.VMEM(squares.shape, jnp.float32),
            pltpu.VMEM((extra, 3 * width), jnp.float32),
        ],
        name="finish",
        compiler_params=pltpu.CompilerParams(vmem_limit_bytes=16 * MIB),
        cost_estimate=pl.CostEstimate(
            flops=10 * rows * width, bytes_accessed=24 * rows * width, transcendentals=0
        ),
    )(*inner, query, keys, grad_q, grad_k, grad_values, squares, gains)


def sum_gains_kernel(*refs):
    groups = refs[:-4]
    half = groups[0].shape[0] // 2
    values = []
    for ref in groups:
        values.append(ref[:half, :].astype(jnp.float32) + ref[half:, :].astype(jnp.float32))
    while len(values) > 1:
        values = [values[i] + values[i + 1] for i in range(0, len(values), 2)]
    total = values[0]
    across = total.shape[1] // HD
    at = 0
    for out in refs[-4:]:
        for j in range(out.shape[1] // HD):
            r, c = at // across, at % across
            out[:, j * HD : (j + 1) * HD] = total[r : r + 1, c * HD : (c + 1) * HD]
            at += 1


def sum_gains(groups, model_width, width):
    extra = gain_row_count(model_width, width)
    at = [group.shape[0] // extra - 1 for group in groups]
    shapes = [(1, model_width), (1, model_width), (1, width), (1, width)]
    outs = pl.pallas_call(
        sum_gains_kernel,
        grid=(1,),
        in_specs=[pl.BlockSpec((extra, 3 * width), lambda i, j=j: (j, 0)) for j in at],
        out_specs=[pl.BlockSpec(shape, lambda i: (0, 0)) for shape in shapes],
        out_shape=[jax.ShapeDtypeStruct(shape, jnp.float32) for shape in shapes],
        name="sum_gains",
        compiler_params=pltpu.CompilerParams(vmem_limit_bytes=4 * MIB),
    )(*groups)
    return [out[0] for out in outs]


def back_product(grad_ref, weights):
    width = weights[0].shape[1]
    return sum(
        times_transposed(grad_ref[:, i * width : (i + 1) * width], weight[...])
        for i, weight in enumerate(weights)
    )


def far_kernel(grad_ref, *refs):
    refs[-1][...] = back_product(grad_ref, refs[:-1]).astype(jnp.bfloat16)


def near_kernel(count, grad_ref, far_ref, *refs):
    own_ref, others = refs[3], refs[4:]
    total = back_product(grad_ref, refs[:3]) + far_ref[...].astype(jnp.float32)
    own_ref[...] = total[:count]
    for k, ref in enumerate(others):
        ref[...] = total[(k + 1) * count : (k + 2) * count].astype(jnp.bfloat16)


def tokens_back(grad, weights, half, part, far=None, count=None):
    depth, width = weights[0].shape
    tile = min(512, depth)
    specs = [pl.BlockSpec((half, 3 * width), lambda j: (part, 0))]
    arrays = [grad]
    if far is not None:
        specs.append(pl.BlockSpec((half, tile), lambda j: (0, j)))
        arrays.append(far)
    specs += [pl.BlockSpec((tile, width), lambda j: (j, 0))] * 3
    if far is None:
        kernel, sizes = far_kernel, [(half, jnp.bfloat16)]
    else:
        kernel = functools.partial(near_kernel, count)
        sizes = [(count, jnp.float32)] + [(count, jnp.bfloat16)] * (half // count - 1)
    return pl.pallas_call(
        kernel,
        grid=(depth // tile,),
        in_specs=specs,
        out_specs=[pl.BlockSpec((size, tile), lambda j: (0, j)) for size, _ in sizes],
        out_shape=[jax.ShapeDtypeStruct((size, depth), kind) for size, kind in sizes],
        name="tokens_back",
        compiler_params=pltpu.CompilerParams(vmem_limit_bytes=16 * MIB),
        cost_estimate=pl.CostEstimate(
            flops=6 * half * depth * width,
            bytes_accessed=6 * depth * width + 8 * half * depth,
            transcendentals=0,
        ),
    )(*arrays, *weights)


def partial_kernel(terms, multiply, count, *refs):
    total = multiply(refs[0][...], refs[terms][...])
    for i in range(1, terms):
        total = total + multiply(refs[i][...], refs[terms + i][...])
    outs = refs[2 * terms :]
    if count is None:
        outs[0][...] = total.astype(jnp.bfloat16)
        return
    total = total + outs[0][...].astype(jnp.float32)
    for k, ref in enumerate(outs[1:]):
        ref[...] = total[k * count : (k + 1) * count].astype(ref.dtype)


def partial_rows(lefts, rights, multiply, part, far=None, kinds=(jnp.bfloat16,)):
    half = lefts[0].shape[0] // 2
    transposed = multiply is times_transposed
    depth = rights[0].shape[0 if transposed else 1]
    tile = min(512, depth)
    if transposed:
        right_specs = [pl.BlockSpec((tile, r.shape[1]), lambda j: (j, 0)) for r in rights]
    else:
        right_specs = [pl.BlockSpec((r.shape[0], tile), lambda j: (0, j)) for r in rights]
    count = None if far is None else half // len(kinds)
    size = count or half
    specs = [
        pl.BlockSpec((half, left.shape[1]), lambda j: (part, 0), pipeline_mode=pl.Buffered(1))
        for left in lefts
    ] + right_specs
    arrays = [*lefts, *rights]
    if far is not None:
        specs.append(pl.BlockSpec((half, tile), lambda j: (0, j)))
        arrays.append(far)
    terms = sum(left.shape[1] for left in lefts)
    return pl.pallas_call(
        functools.partial(partial_kernel, len(lefts), multiply, count),
        grid=(depth // tile,),
        in_specs=specs,
        out_specs=[pl.BlockSpec((size, tile), lambda j: (0, j)) for _ in kinds],
        out_shape=[jax.ShapeDtypeStruct((size, depth), kind) for kind in kinds],
        name="partial_rows",
        compiler_params=pltpu.CompilerParams(vmem_limit_bytes=14 * MIB),
        cost_estimate=pl.CostEstimate(
            flops=2 * half * depth * terms,
            bytes_accessed=2 * terms * (half + depth) + 6 * half * depth,
            transcendentals=0,
        ),
    )(*arrays)


def out_grad_kernel(pieces, *refs):
    attended_ref, me_ref = refs[pieces : pieces + 2]
    own_ref, others, grad_ref = refs[pieces + 2], refs[pieces + 3 : -1], refs[-1]
    count = own_ref.shape[0]
    grad_ref[...] = transposed_times(attended_ref[...], joined(refs[:pieces]))
    me = me_ref[0]
    own_ref[...] = grad_ref[pl.ds(pl.multiple_of(me * count, count), count), :]
    for j, ref in enumerate(others):
        start = pl.multiple_of((me ^ (j + 1)) * count, count)
        ref[...] = grad_ref[pl.ds(start, count), :].astype(jnp.bfloat16)


def out_grad(attended, grad_attn, me, dp_size):
    width, depth = attended.shape[1], grad_attn[0].shape[1]
    piece = (width // dp_size, depth)
    return pl.pallas_call(
        functools.partial(out_grad_kernel, len(grad_attn)),
        in_specs=[pl.BlockSpec(array.shape, lambda: (0, 0)) for array in (*grad_attn, attended)]
        + [pl.BlockSpec(memory_space=pltpu.SMEM)],
        out_shape=[jax.ShapeDtypeStruct(piece, jnp.float32)]
        + [jax.ShapeDtypeStruct(piece, jnp.bfloat16)] * (dp_size - 1),
        scratch_shapes=[pltpu.VMEM((width, depth), jnp.float32)],
        name="out_grad",
        compiler_params=pltpu.CompilerParams(vmem_limit_bytes=16 * MIB),
        cost_estimate=pl.CostEstimate(
            flops=2 * attended.shape[0] * width * depth,
            bytes_accessed=2 * attended.shape[0] * (width + depth) + 3 * width * depth,
            transcendentals=0,
        ),
    )(*[in_hbm(piece) for piece in grad_attn], attended, me)


def assemble_kernel(*refs):
    me = refs[-2][0]
    out_ref = refs[-1]
    for j, ref in enumerate(refs[:-2]):
        count = ref.shape[0]
        start = pl.multiple_of((me ^ j) * count, count)
        out_ref[pl.ds(start, count), :] = ref[...].astype(jnp.float32)


def assemble(pieces, me):
    count, depth = pieces[0].shape
    return pl.pallas_call(
        assemble_kernel,
        in_specs=[pl.BlockSpec((count, depth), lambda: (0, 0)) for _ in pieces]
        + [pl.BlockSpec(memory_space=pltpu.SMEM)],
        out_shape=jax.ShapeDtypeStruct((len(pieces) * count, depth), jnp.float32),
        name="assemble",
        compiler_params=pltpu.CompilerParams(vmem_limit_bytes=8 * MIB),
    )(*pieces, me)


def summed_blocks(refs, orders):
    rows = []
    for i in range(refs[0].shape[0]):
        total = refs[0][i : i + 1, :]
        for order, other in zip(orders, refs[1:]):
            total = total + other[order[i] : order[i] + 1, :]
        rows.append(total)
    return rows


def add_blocks_kernel(orders, *refs):
    own, others, out = refs[0], refs[1:-1], refs[-1]
    count = len(orders[0])
    for i in range(count):
        total = own[i : i + 1, :]
        for order, other in zip(orders, others):
            total = total + other[order[i] : order[i] + 1, :]
        out[i : i + 1, :] = total
    if own.shape[0] > count:
        rest = [own[count:, :]] + [other[count:, :] for other in others]
        while len(rest) > 1:
            rest = [rest[i] + rest[i + 1] for i in range(0, len(rest), 2)]
        out[count:, :] = rest[0]


def add_pieces_kernel(*refs):
    total = refs[0][...]
    for ref in refs[1:-1]:
        total = total + ref[...].astype(jnp.float32)
    refs[-1][...] = total.astype(jnp.bfloat16)


def add_pieces(own, others):
    return pl.pallas_call(
        add_pieces_kernel,
        out_shape=jax.ShapeDtypeStruct(own.shape, jnp.bfloat16),
        name="add_pieces",
        compiler_params=pltpu.CompilerParams(vmem_limit_bytes=4 * MIB),
    )(own, *others)


def add_blocks(own, others, orders):
    return pl.pallas_call(
        functools.partial(add_blocks_kernel, orders),
        out_shape=jax.ShapeDtypeStruct(own.shape, own.dtype),
        name="add_blocks",
        compiler_params=pltpu.CompilerParams(vmem_limit_bytes=4 * MIB),
    )(own, *others)


def in_hbm(array):
    return pltpu.with_memory_space_constraint(array, pltpu.HBM)


def resident(shape):
    return pl.BlockSpec(shape, lambda i: (0, 0), pipeline_mode=pl.Buffered(1))


def joined(refs):
    return refs[0][...] if len(refs) == 1 else jnp.concatenate([r[...] for r in refs], axis=0)


def project_kernel(pieces, *refs):
    rows = joined(refs[:pieces])
    w_query_ref, w_key_ref, w_value_ref, query_ref, keys_ref, values_ref, squares_ref = refs[
        pieces:
    ]
    blocks = list(range(squares_ref.shape[0]))
    count = rows.shape[0] // len(blocks)
    if 2 * count < squares_ref.shape[1]:
        squares_ref[...] = jnp.zeros_like(squares_ref)
    for i, weight, out in ((0, w_query_ref, query_ref), (1, w_key_ref, keys_ref)):
        value = product(rows, weight[...])
        out[...] = value
        square = value * value
        folded = square[:, :HD]
        for h in range(1, value.shape[1] // HD):
            folded = folded + square[:, h * HD : (h + 1) * HD]
        store_blocks(squares_ref, i, blocks, row_sums(folded), count)
    values_ref[...] = product(rows, w_value_ref[...]).astype(jnp.bfloat16)


def project(rows, w_query, w_key, w_value, tensor_size):
    count = sum(piece.shape[0] for piece in rows)
    depth, width = w_query.shape
    wide = jax.ShapeDtypeStruct((count, width), jnp.float32)
    return pl.pallas_call(
        functools.partial(project_kernel, len(rows)),
        out_shape=(
            wide,
            wide,
            jax.ShapeDtypeStruct((count, width), jnp.bfloat16),
            jax.ShapeDtypeStruct((tensor_size, max(HD, 2 * count // tensor_size)), jnp.float32),
        ),
        name="project",
        compiler_params=pltpu.CompilerParams(vmem_limit_bytes=16 * MIB),
        cost_estimate=pl.CostEstimate(
            flops=6 * count * depth * width,
            bytes_accessed=2 * count * depth + 6 * depth * width + 10 * count * width,
            transcendentals=0,
        ),
    )(*[in_hbm(array) for array in (*rows, w_query, w_key, w_value)])


def ffn_kernel(pieces, *refs):
    rows = joined(refs[:pieces])
    w_gate_ref, w_up_ref, gate_ref, up_ref, swiglu_ref = refs[pieces:]
    gate = product(rows, w_gate_ref[...])
    up = product(rows, w_up_ref[...])
    gate_ref[...] = gate.astype(jnp.bfloat16)
    up_ref[...] = up.astype(jnp.bfloat16)
    swiglu_ref[...] = (gate * jax.nn.sigmoid(gate) * up).astype(jnp.bfloat16)


def ffn(rows, w_gate, w_up):
    count = sum(piece.shape[0] for piece in rows)
    depth, units = w_gate.shape
    tile = min(256, units)
    weight = pl.BlockSpec((depth, tile), lambda j: (0, j))
    out = pl.BlockSpec((count, tile), lambda j: (0, j))
    wide = jax.ShapeDtypeStruct((count, units), jnp.bfloat16)
    return pl.pallas_call(
        functools.partial(ffn_kernel, len(rows)),
        grid=(units // tile,),
        in_specs=[resident(piece.shape) for piece in rows]
        + [weight, weight],
        out_specs=(out, out, out),
        out_shape=(wide, wide, jax.ShapeDtypeStruct((count, units), jnp.bfloat16)),
        name="ffn",
        compiler_params=pltpu.CompilerParams(vmem_limit_bytes=16 * MIB),
        cost_estimate=pl.CostEstimate(
            flops=4 * count * depth * units,
            bytes_accessed=2 * count * depth + 4 * depth * units + 10 * count * units,
            transcendentals=count * units,
        ),
    )(*rows, w_gate, w_up)


def ffn_back_kernel(pieces, *refs):
    grad = joined(refs[:pieces])
    w_down_ref, gate_ref, up_ref, grad_gate_ref, grad_up_ref = refs[pieces:]
    grad_swiglu = times_transposed(grad, w_down_ref[...])
    gate = gate_ref[...].astype(jnp.float32)
    sig = jax.nn.sigmoid(gate)
    grad_gate = grad_swiglu * up_ref[...].astype(jnp.float32) * sig * (1.0 + gate * (1.0 - sig))
    grad_gate_ref[...] = grad_gate.astype(jnp.bfloat16)
    grad_up_ref[...] = (grad_swiglu * (gate * sig)).astype(jnp.bfloat16)


def ffn_back(grad, w_down, gate, up, place=lambda array: array):
    count = sum(piece.shape[0] for piece in grad)
    units, depth = w_down.shape
    tile = min(256, units)
    out = pl.BlockSpec((count, tile), lambda j: (0, j))
    narrow = jax.ShapeDtypeStruct((count, units), jnp.bfloat16)
    return pl.pallas_call(
        functools.partial(ffn_back_kernel, len(grad)),
        grid=(units // tile,),
        in_specs=[resident(piece.shape) for piece in grad]
        + [pl.BlockSpec((tile, depth), lambda j: (j, 0)), out, out],
        out_specs=(out, out),
        out_shape=(narrow, narrow),
        name="ffn_back",
        compiler_params=pltpu.CompilerParams(vmem_limit_bytes=16 * MIB),
        cost_estimate=pl.CostEstimate(
            flops=2 * count * depth * units,
            bytes_accessed=2 * count * depth + 2 * depth * units + 12 * count * units,
            transcendentals=count * units,
        ),
    )(*grad, *[place(array) for array in (w_down, gate, up)])


def weight_grad_kernel(left_counts, right_counts, rights, outs, *refs):
    groups = len(left_counts)
    left, at = [], 0
    for count in left_counts:
        left.append(joined(refs[at : at + count]))
        at += count
    out_refs = refs[len(refs) - rights * outs :]
    for r in range(rights):
        right = []
        for count in right_counts:
            right.append(refs[at : at + count])
            at += count
        width = right[0][0].shape[1] // outs
        for o in range(outs):
            sums = []
            for g in range(groups):
                pieces = [ref[:, o * width : (o + 1) * width] for ref in right[g]]
                whole = pieces[0] if len(pieces) == 1 else jnp.concatenate(pieces, axis=0)
                sums.append(transposed_times(left[g], whole))
            while len(sums) > 1:
                sums = [sums[i] - sums[i + 1] * -1.0 for i in range(0, len(sums), 2)]
            out_refs[r * outs + o][...] = sums[0]


def weight_grad(left, *rights, outs=1, extra=0):
    depth = left[0][0].shape[1]
    left_pieces = [piece for group in left for piece in group]
    right_pieces, counts = [], []
    for right in rights:
        for group in right:
            right_pieces += group
            counts += [piece.shape[0] for piece in group[:-1]] + [group[-1].shape[0] - extra]
    rows = sum(piece.shape[0] for piece in left_pieces)
    widths = [right[0][0].shape[1] // outs for right in rights for _ in range(outs)]
    tile = min(256, depth)
    blocks = 4 * rows * tile + (2 * len(rights)) * rows * rights[0][0][0].shape[1]
    needed = blocks + 4 * tile * sum(widths) * (2 + len(left)) + 4 * MIB
    return pl.pallas_call(
        functools.partial(
            weight_grad_kernel,
            [len(group) for group in left],
            [len(group) for group in rights[0]],
            len(rights),
            outs,
        ),
        grid=(depth // tile,),
        in_specs=[pl.BlockSpec((piece.shape[0], tile), lambda i: (0, i)) for piece in left_pieces]
        + [
            resident((count, piece.shape[1])) for count, piece in zip(counts, right_pieces)
        ],
        out_specs=[pl.BlockSpec((tile, width), lambda i: (i, 0)) for width in widths],
        out_shape=[jax.ShapeDtypeStruct((depth, width), jnp.float32) for width in widths],
        name="weight_grad",
        compiler_params=pltpu.CompilerParams(vmem_limit_bytes=max(28 * MIB, needed)),
        cost_estimate=pl.CostEstimate(
            flops=2 * rows * depth * sum(widths),
            bytes_accessed=2 * rows * (depth + sum(widths)) + 4 * depth * sum(widths),
            transcendentals=0,
        ),
    )(*[in_hbm(piece) for piece in left_pieces], *right_pieces)


def build(dp_size, tensor_size):
    pairs = tensor_size // 2

    def swap(value, axis, mask):
        size = dp_size if axis == "dp" else tensor_size
        return lax.ppermute(value, axis, [(i, i ^ mask) for i in range(size)])

    def tensor_gather(own, relay=False):
        near = [own]
        for k in range(1, pairs):
            if relay and k == 3:
                near.append(swap(near[2], "tensor", 2))
            else:
                near.append(swap(own, "tensor", 2 * k))
        return near + [swap(near[k], "tensor", 1) for k in range(pairs)]

    def tensor_scatter(partial_of, rows, relay=False):
        half = rows // 2
        far = partial_of(half, rows).astype(jnp.bfloat16)
        far = swap(far, "tensor", 1)
        near = partial_of(0, half) + far.astype(jnp.float32)
        count = half // pairs
        total = near[:count]
        if relay and pairs == 4:
            one, two, three = [near[k * count : (k + 1) * count] for k in range(1, pairs)]
            three = swap(three.astype(jnp.bfloat16), "tensor", 2)
            one = swap(one.astype(jnp.bfloat16), "tensor", 2)
            two = (two + three.astype(jnp.float32)).astype(jnp.bfloat16)
            two = swap(two, "tensor", 4)
            return total + one.astype(jnp.float32) + two.astype(jnp.float32)
        for k in range(1, pairs):
            block = near[k * count : (k + 1) * count].astype(jnp.bfloat16)
            total = total + swap(block, "tensor", 2 * k).astype(jnp.float32)
        return total

    def product_scatter(lefts, rights, multiply):
        (far,) = partial_rows(lefts, rights, multiply, 1)
        far = swap(far, "tensor", 1)
        relay = pairs == 4
        kinds = [jnp.float32] + [jnp.bfloat16] * (pairs - 1)
        if relay:
            kinds[2] = jnp.float32
        total, *blocks = partial_rows(lefts, rights, multiply, 0, far, tuple(kinds))
        if relay:
            three = swap(blocks[2], "tensor", 2).astype(jnp.float32)
            one = swap(blocks[0], "tensor", 2).astype(jnp.float32)
            two = swap((blocks[1] + three).astype(jnp.bfloat16), "tensor", 4)
            return total + one + two.astype(jnp.float32)
        for k, block in enumerate(blocks):
            total = total + swap(block, "tensor", 2 * k + 2).astype(jnp.float32)
        return total

    def row_sum(value):
        def order(mask):
            out = []
            for i in range(tensor_size):
                wanted = (2 * (i % pairs) + i // pairs) ^ mask
                out.append((wanted % 2) * pairs + wanted // 2)
            return out

        value = add_blocks(value, [swap(value, "tensor", 1)], [order(1)])
        others = [swap(value, "tensor", 2 * k) for k in range(1, pairs)]
        return [value] + others, [order(2 * k) for k in range(1, pairs)]

    def dp_gather(own, cut):
        if dp_size == 4:
            one = swap(own, "dp", 1)
            two = swap(own, "dp", 2)
            top = one[:cut]
            bottom = two[cut:]
            top = swap(top, "dp", 2)
            bottom = swap(bottom, "dp", 1)
            return [[own], [one], [two], [top, bottom]]
        return [[own]] + [[swap(own, "dp", j)] for j in range(1, dp_size)]

    def dp_gather_shared(pieces):
        near = jnp.concatenate(pieces[:pairs], axis=0)
        fetched = dp_gather(near, near.shape[0] // 2)[1:]
        groups = [[near] + pieces[pairs:]]
        for mine in fetched:
            groups.append(mine + [swap(piece, "tensor", 1) for piece in mine])
        return groups

    def dp_sum(own, others, me):
        others = [swap(piece, "dp", j + 1) for j, piece in enumerate(others)]
        total = add_pieces(own, others)
        pieces = [total] + [swap(total, "dp", j) for j in range(1, dp_size)]
        return assemble(pieces, me)

    def positions(rows):
        count = rows // tensor_size
        index = jnp.arange(rows, dtype=jnp.int32)
        block = index // count
        mask = 2 * (block % pairs) + block // pairs
        owner = lax.axis_index("tensor").astype(jnp.int32) ^ mask
        return (owner * count + index % count) % SEQ

    def tables_of(rows):
        pos = positions(rows)
        half_width = HD // 2
        exponent = jnp.arange(half_width, dtype=jnp.float32) * (2.0 / HD)
        frequency = rope_base ** (-exponent)
        angles = pos.astype(jnp.float32)[:, None] * frequency[None, :]
        cos, sin = jnp.cos(angles), jnp.sin(angles)
        return (
            jnp.concatenate([cos, cos], axis=1),
            jnp.concatenate([-sin, sin], axis=1),
            pos[None, :],
        )

    def shards(
        tokens,
        cotangent,
        w_query,
        w_key,
        w_value,
        w_out,
        w_gate,
        w_up,
        w_down,
        q_gain,
        k_gain,
        attn_gain,
        ffn_gain,
    ):
        model_width = tokens.shape[1]
        rows = tokens.shape[0] * tensor_size
        width = w_query.shape[1]
        tables = tables_of(rows)

        gathered = tensor_gather(tokens, relay=True)
        query, keys, values, squares = project(gathered, w_query, w_key, w_value, tensor_size)
        square_parts, orders = row_sum(squares)
        attended, q_rot, k_rot, squares = attend(
            query, keys, values, square_parts, orders, q_gain, k_gain, tables, model_width
        )
        attn_rows = tensor_scatter(lambda a, b: product(attended[a:b], w_out), rows, relay=True)
        a_inverse = row_scale(attn_rows)
        a_normed = attn_rows * a_inverse
        mixed = tokens.astype(jnp.float32) + a_normed * attn_gain
        mixed_b = tensor_gather(mixed.astype(jnp.bfloat16), relay=True)
        gate, up_proj, swiglu = ffn(mixed_b, w_gate, w_up)
        ffn_rows = tensor_scatter(lambda a, b: product(swiglu[a:b], w_down), rows, relay=True)
        m_inverse = row_scale(ffn_rows)
        m_normed = ffn_rows * m_inverse
        layer_out = mixed + m_normed * ffn_gain
        grad_out = cotangent.astype(jnp.float32)
        ffn_gain_part = jnp.sum(grad_out * m_normed, axis=0)
        grad_ffn = tensor_gather(
            norm_back(grad_out * ffn_gain, m_normed, m_inverse).astype(jnp.bfloat16), relay=True
        )
        grad_gate, grad_up = ffn_back(grad_ffn, w_down, gate, up_proj)
        grad_mixed = grad_out + product_scatter(
            [grad_gate, grad_up], [w_gate, w_up], times_transposed
        )
        attn_gain_part = jnp.sum(grad_mixed * a_normed, axis=0)
        grad_attn = tensor_gather(
            norm_back(grad_mixed * attn_gain, a_normed, a_inverse).astype(jnp.bfloat16), relay=True
        )
        me = lax.axis_index("dp").astype(jnp.int32).reshape(1)
        grad_values, grad_q, grad_k, inner, gain_parts = attend_back(
            grad_attn,
            w_out,
            q_rot,
            k_rot,
            values,
            query,
            keys,
            squares,
            q_gain,
            k_gain,
            tables,
            model_width,
        )
        lanes = inner.shape[1]
        inner_parts, orders = row_sum(
            jnp.concatenate(
                [inner, attn_gain_part.reshape(-1, lanes), ffn_gain_part.reshape(-1, lanes)]
            ),
        )
        out_own, *out_others = out_grad(attended, grad_attn, me, dp_size)
        grad_qkv = finish(
            query,
            keys,
            grad_q,
            grad_k,
            grad_values,
            squares,
            inner_parts,
            gain_parts,
            orders,
            model_width,
        )
        weights = (w_query, w_key, w_value)
        (far,) = tokens_back(grad_qkv, weights, rows // 2, 1)
        far = swap(far, "tensor", 1)
        own, *others = tokens_back(
            grad_qkv, weights, rows // 2, 0, far, tokens.shape[0]
        )
        others = [swap(piece, "tensor", 2 * k + 2) for k, piece in enumerate(others)]
        grad_tokens = grad_mixed + sum([piece.astype(jnp.float32) for piece in others], own)

        tokens_all = dp_gather_shared(gathered)
        mixed_all = dp_gather_shared(mixed_b)
        grad_ffn_all = dp_gather_shared(grad_ffn)
        swiglus, grad_gates, grad_ups = [[swiglu]], [[grad_gate]], [[grad_up]]
        for j in range(1, dp_size):
            gate_j, up_j, swiglu_j = ffn(mixed_all[j], w_gate, w_up)
            grad_gate_j, grad_up_j = ffn_back(
                grad_ffn_all[j], w_down, gate_j, up_j, *[in_hbm][: j // (dp_size - 1)]
            )
            swiglus.append([swiglu_j])
            grad_gates.append([grad_gate_j])
            grad_ups.append([grad_up_j])
        (grad_w_down,) = weight_grad(swiglus, grad_ffn_all)
        (grad_w_gate,) = weight_grad(mixed_all, grad_gates)
        (grad_w_up,) = weight_grad(mixed_all, grad_ups)
        grad_w_out = dp_sum(out_own, out_others, me)
        operands = dp_gather(grad_qkv, rows // 2)
        grad_w_query, grad_w_key, grad_w_value = weight_grad(
            tokens_all, operands, outs=3, extra=grad_qkv.shape[0] - rows
        )
        gains = sum_gains([group[-1] for group in operands], model_width, width)
        return (
            layer_out,
            grad_tokens,
            grad_w_query,
            grad_w_key,
            grad_w_value,
            grad_w_out,
            grad_w_gate,
            grad_w_up,
            grad_w_down,
            gains[2],
            gains[3],
            gains[0],
            gains[1],
        )

    return shards


def solution(mesh):
    placed = (
        P(("dp", "tensor"), None),
        P(("dp", "tensor"), None),
        P(None, "tensor"),
        P(None, "tensor"),
        P(None, "tensor"),
        P("tensor", None),
        P(None, "tensor"),
        P(None, "tensor"),
        P("tensor", None),
        P("tensor"),
        P("tensor"),
        P(),
        P(),
    )
    return jax.shard_map(
        build(mesh.shape["dp"], mesh.shape["tensor"]),
        mesh=mesh,
        in_specs=placed,
        out_specs=(
            P(("dp", "tensor"), None),
            P(("dp", "tensor"), None),
            P(None, "tensor"),
            P(None, "tensor"),
            P(None, "tensor"),
            P("tensor", None),
            P(None, "tensor"),
            P(None, "tensor"),
            P("tensor", None),
            P("tensor"),
            P("tensor"),
            P(),
            P(),
        ),
        check_vma=False,
    )
```
